128 devices in a mesh: replica: 8 (over z_hi, y), tensor: 16 (over x, z_lo, core).
Axes of the slice: x: 4, y: 4, z: 4 (z_hi: 2, z_lo: 2; z = z_hi * 2 + z_lo), core: 2. Of those that a mesh axis runs over, the one named last changes fastest.
Arguments:
- queries: bfloat16 [1024, 8192], P('replica', 'tensor'), may hold values from -200 to 200
- new_kv: bfloat16 [1024, 1024], P('replica'), may hold values from -8 to 8
- kv_pool: bfloat16 [1024, 64, 1024], P(('replica', 'tensor')), may hold values from -6 to 6
- anchor: int32 [8, 8], replicated, may hold values from 0 to 7, as said below
- page_table: int32 [64, 16], replicated, may hold values from 0 to 7, as said below
- prefix_len: int32 [64], replicated, may hold values from 1 to 1024, 32768 in all
- turn_rows: int32 [8, 8], replicated, may hold values from 1 to 32, 128 in all within a row
- out_weight: bfloat16 [8192, 16384], P('tensor', 'replica'), may hold values from -0.5 to 0.5
- residual: bfloat16 [1024, 16384], P(None, 'replica'), may hold values from -400 to 400
- norm_gain: bfloat16 [16384], P('replica'), may hold values from 0.099609375 to 1.8984375
- gate_up: bfloat16 [16384, 2, 26624], P('replica', None, 'tensor'), may hold values from -0.046875 to 0.046875
Outputs:
- hidden: bfloat16 [1024, 26624], P('replica', 'tensor')
The draws below stay inside these ranges and needn't reach their ends.
Inputs may be any that keep to these rules, and one draw needn't show every extreme that they name: Slot j of new replica d holds session anchor[d, j] of old replica j; for each old replica, the 8 slots that come from it name each of its 8 sessions exactly once. `page_table`: row o * 8 + s lists the pages of session s of old replica o: entry k is a local page index on device k of that replica's 16 tensor devices, whose pages are numbered (o * 16 + k) * 8 + index in kv_pool; on each device the 8 sessions use distinct pages. `prefix_len`: indexed by d * 8 + j for slot j of new replica d. `turn_rows`: each replica's entries sum to 128.
All inputs are finite; a program needn't handle non-finite values.
Results may differ from the reference program's by a relative error of at most 0.0064.
Values may be sent and summed in bfloat16 or wider, within the bound.
A program may use at most 128 MiB of HBM per device.

```python
import math
import jax
import jax.numpy as jnp
import numpy as np
from jax import lax

D = 16384
HD = 128
HEADS = 64
KVH = 4
FF = 26624
PAGE = 64
SHARE = 1
ROWS = 128
REPLICAS = 8
SR = 8
MAXP = 16
GROUP = 16


def draw_anchor(key, part):
    keys = jax.random.split(jax.random.fold_in(key, 3), REPLICAS)
    orders = jax.vmap(lambda single: jax.random.permutation(single, SR))(keys)
    table = orders.reshape(REPLICAS, REPLICAS, SHARE)
    return jnp.transpose(table, (1, 0, 2)).reshape(REPLICAS, SR).astype(jnp.int32)


def draw_page_table(key, part):
    keys = jax.random.split(jax.random.fold_in(key, 7), REPLICAS * MAXP)
    orders = jax.vmap(lambda single: jax.random.permutation(single, SR))(keys)
    table = jnp.transpose(orders.reshape(REPLICAS, MAXP, SR), (0, 2, 1))
    return table.reshape(REPLICAS * SR, MAXP).astype(jnp.int32)


def attention_inputs(key):
    total_rows = REPLICAS * ROWS
    key_draw = jnp.clip(jax.random.normal(jax.random.fold_in(key, 21), (total_rows, KVH, 2, HD), jnp.float32), -6.0, 6.0)
    query_draw = jnp.clip(jax.random.normal(jax.random.fold_in(key, 22), (total_rows, KVH, GROUP, HD), jnp.float32), -6.0, 6.0)
    return (query_draw.reshape(total_rows, HEADS * HD), key_draw.reshape(total_rows, KVH * 2 * HD))


def draw_queries(key, part):
    return attention_inputs(key)[0].astype(jnp.bfloat16)


def draw_new_kv(key, part):
    return attention_inputs(key)[1].astype(jnp.bfloat16)


def draw_residual(key, part):
    total_rows = REPLICAS * ROWS
    row_scale = 10.0 ** jax.random.uniform(jax.random.fold_in(key, 31), (total_rows, 1), jnp.float32)
    column_pos = jnp.arange(D, dtype=jnp.float32)[None, :] / D
    column_scale = 10.0 ** (0.5 * jax.random.uniform(jax.random.fold_in(key, 32), (1, D), jnp.float32) + 0.5 * column_pos)
    base = jnp.clip(jax.random.normal(jax.random.fold_in(key, 34), (total_rows, D), jnp.float32), -6.0, 6.0)
    return (0.3 * base * row_scale * column_scale).astype(jnp.bfloat16)


def level_of(stream_key, shape, cuts, smallest, top_value):
    def one(axis_at, parts):
        heights = jax.random.uniform(jax.random.fold_in(jax.random.fold_in(stream_key, 6), axis_at), (parts,), jnp.float32, smallest / len(cuts), top_value / len(cuts))
        return jnp.repeat(jnp.exp(heights), shape[axis_at] // parts).reshape((-1,) + (1,) * (len(shape) - axis_at - 1))

    factor_of = one(*cuts[0])
    for cut in cuts[1:]:
        factor_of = factor_of * one(*cut)
    return factor_of


def length_profile(number_of, total, reach, lean):
    weights = [(1 << 20) // math.isqrt(rank ** lean) + 1 for rank in range(2, number_of + 1)]
    spare, given = total - reach - (number_of - 1), [1] * (number_of - 1)
    while spare > 0:
        movable = [i for i in range(number_of - 1) if given[i] < reach]
        whole, remaining = sum([weights[i] for i in movable]), spare
        for i in movable:
            addition = min(reach - given[i], max(1, remaining * weights[i] // whole), spare)
            given[i] = given[i] + addition
            spare = spare - addition
    return np.array([reach] + given)


def ragged(own_key, amount, total, most, slope):
    if amount == 2:
        one = jax.random.randint(own_key, (), max(1, total - most), min(most, total - 1) + 1)
        return jnp.stack([one, total - one])
    sizes = jnp.asarray(length_profile(amount, total, most, slope), jnp.int32)
    couples = (amount - 1) // 2
    donor, taker = sizes[1:1 + 2 * couples:2], sizes[2:2 + 2 * couples:2]
    room = jnp.minimum(donor - 1, most - taker)
    passed = jax.random.randint(jax.random.fold_in(own_key, 1), (couples,), 0, 1 << 20) % (room + 1)
    sizes = sizes.at[1:1 + 2 * couples:2].set(donor - passed).at[2:2 + 2 * couples:2].set(taker + passed)
    return sizes[jax.random.permutation(jax.random.fold_in(own_key, 2), amount)]


def normal_values(own_key, dims, deviation, bound, cuts=(), kind=jnp.bfloat16):
    level = level_of(own_key, dims, cuts, -0.22, 0.18) if cuts else 1.0
    values = jax.random.normal(own_key, dims, jnp.float32) * deviation * level
    return jnp.minimum(jnp.maximum(values, -bound), bound).astype(kind)


def setup_inputs(seed: int = 0) -> dict:
    key_list = jax.random.split(jax.random.key(seed), 12)
    queries = draw_queries(jax.random.fold_in(key_list[11], 71), 0)
    new_kv = draw_new_kv(jax.random.fold_in(key_list[11], 71), 0)
    kv_pool = normal_values(key_list[2], (REPLICAS * MAXP * SR, PAGE, KVH * 2 * HD), 1.0, 6.0, ((0, 128),))
    anchor = draw_anchor(jax.random.fold_in(key_list[11], 71), 0)
    page_table = draw_page_table(jax.random.fold_in(key_list[11], 71), 0)
    prefix_len = ragged(key_list[5], REPLICAS * SR, REPLICAS * SR * MAXP * PAGE // 2, MAXP * PAGE, 2).astype(jnp.int32)
    turn_rows = jax.vmap(lambda own: ragged(own, SR, ROWS, ROWS // 4, 2))(jax.random.split(key_list[6], REPLICAS)).reshape((REPLICAS, SR)).astype(jnp.int32)
    out_weight = normal_values(key_list[7], (HEADS * HD, D), HD ** -0.5, 0.5, ((0, 16), (1, 8)))
    residual = draw_residual(jax.random.fold_in(key_list[11], 71), 0)
    norm_gain = jnp.clip(1.0 + 0.18 * jax.random.normal(key_list[9], (D,), jnp.float32), 0.099609375, 1.8984375).astype(jnp.bfloat16)
    gate_up = normal_values(key_list[10], (D, 2, FF), D ** -0.5, 0.046875, ((0, 8), (2, 16)))
    return {"queries": queries, "new_kv": new_kv, "kv_pool": kv_pool, "anchor": anchor, "page_table": page_table, "prefix_len": prefix_len, "turn_rows": turn_rows, "out_weight": out_weight, "residual": residual, "norm_gain": norm_gain, "gate_up": gate_up}


EPSILON = 1e-05

def reference(queries, new_kv, kv_pool, anchor, page_table, prefix_len, turn_rows, out_weight, residual, norm_gain, gate_up):
    cached_len = MAXP * PAGE
    slot_ids = jnp.arange(SR, dtype=jnp.int32)
    old_replica = slot_ids // SHARE
    page_cols = jnp.arange(MAXP, dtype=jnp.int32)
    score_scale = HD ** (-0.5)

    def one_replica(replica_id):
        old_session = old_replica * SR + jnp.take(anchor, replica_id, axis=0)
        table = jnp.take(page_table, old_session, axis=0)
        page_ids = (old_replica[:, None] * MAXP + page_cols[None, :]) * SR + table
        cached_pages = jnp.take(kv_pool, page_ids.reshape(-1), axis=0)
        cached_pages = cached_pages.reshape(SR * cached_len, KVH, 2, HD).astype(jnp.float32)
        query_block = lax.dynamic_slice_in_dim(queries, replica_id * ROWS, ROWS, 0)
        query_block = query_block.reshape(ROWS, KVH, GROUP, HD).astype(jnp.float32)
        fresh_pairs = lax.dynamic_slice_in_dim(new_kv, replica_id * ROWS, ROWS, 0)
        fresh_pairs = fresh_pairs.reshape(ROWS, KVH, 2, HD).astype(jnp.float32)
        counts = jnp.take(turn_rows, replica_id, axis=0)
        bounds = jnp.cumsum(counts, dtype=jnp.int32)
        row_ids = jnp.arange(ROWS, dtype=jnp.int32)
        row_slot = lax.optimization_barrier(jnp.sum((row_ids[:, None] >= bounds[None, :]).astype(jnp.int32), axis=1, dtype=jnp.int32))
        lengths = lax.dynamic_slice_in_dim(prefix_len, replica_id * SR, SR, 0)
        key_ids = jnp.arange(SR * cached_len, dtype=jnp.int32)
        key_slot = key_ids // cached_len
        key_pos = key_ids % cached_len
        length_limit = jnp.repeat(lengths, cached_len)
        prefix_mask = (key_slot[None, :] == row_slot[:, None]) & (key_pos[None, :] < length_limit[None, :])
        fresh_mask = (row_slot[None, :] == row_slot[:, None]) & (row_ids[None, :] <= row_ids[:, None])
        prefix_scores = jnp.einsum('rgqd,kgd->gqrk', query_block, cached_pages[:, :, 0, :]) * score_scale
        fresh_scores = jnp.einsum('rgqd,kgd->gqrk', query_block, fresh_pairs[:, :, 0, :]) * score_scale
        prefix_scores = jnp.where(prefix_mask[None, None], prefix_scores, -jnp.inf)
        fresh_scores = jnp.where(fresh_mask[None, None], fresh_scores, -jnp.inf)
        row_peak = jnp.maximum(lax.optimization_barrier(jnp.max(prefix_scores, axis=3)), lax.optimization_barrier(jnp.max(fresh_scores, axis=3)))
        prefix_weights = jnp.exp(prefix_scores - row_peak[..., None])
        fresh_weights = jnp.exp(fresh_scores - row_peak[..., None])
        denominator = lax.optimization_barrier(jnp.sum(prefix_weights, axis=3)) + lax.optimization_barrier(jnp.sum(fresh_weights, axis=3))
        prefix_rounded = lax.optimization_barrier(prefix_weights.astype(jnp.bfloat16)).astype(jnp.float32)
        fresh_rounded = lax.optimization_barrier(fresh_weights.astype(jnp.bfloat16)).astype(jnp.float32)
        mixed_values = jnp.einsum('gqrk,kgd->rgqd', prefix_rounded, cached_pages[:, :, 1, :])
        mixed_values = mixed_values + jnp.einsum('gqrk,kgd->rgqd', fresh_rounded, fresh_pairs[:, :, 1, :])
        mixed_values = mixed_values / jnp.transpose(denominator, (2, 0, 1))[..., None]
        return mixed_values.reshape(ROWS, HEADS * HD).astype(jnp.bfloat16)
    attended = lax.map(one_replica, jnp.arange(REPLICAS, dtype=jnp.int32))
    attended = attended.reshape(REPLICAS * ROWS, HEADS * HD)
    carried = residual.astype(jnp.float32) + jnp.dot(attended, out_weight, preferred_element_type=jnp.float32)
    inv_rms = lax.rsqrt(lax.optimization_barrier(jnp.sum(carried * carried, axis=1)) / D + EPSILON)
    normed = (carried * inv_rms[:, None] * norm_gain.astype(jnp.float32)[None, :]).astype(jnp.bfloat16)
    gate = jnp.dot(normed, gate_up[:, 0, :], preferred_element_type=jnp.float32)
    up_part = jnp.dot(normed, gate_up[:, 1, :], preferred_element_type=jnp.float32)
    return (jax.nn.silu(gate) * up_part).astype(jnp.bfloat16)
```

```python
import jax
import jax.numpy as jnp
import numpy as np
from jax import lax
from jax.sharding import PartitionSpec as P

D = 16384
HD = 128
HEADS = 64
KVH = 4
PAGE = 64
SHARE = 1
ROWS = 128
GROUP = 16


EPSILON = 1e-05


def per_device(
    queries,
    new_kv,
    kv_pool,
    anchor,
    page_table,
    prefix_len,
    turn_rows,
    out_weight,
    residual,
    norm_gain,
    gate_up,
):
    replicas = lax.axis_size("replica")
    tensors = lax.axis_size("tensor")
    replica_idx = lax.axis_index("replica")
    tensor_idx = lax.axis_index("tensor")
    sessions = SHARE * replicas
    heads_local = HEADS // tensors
    pair_width = 2 * HD
    cached_len = tensors * PAGE
    owner_head = np.arange(tensors) * heads_local // GROUP
    from_here = lax.dynamic_slice_in_dim(anchor, replica_idx * SHARE, SHARE, 1)
    table_rows = lax.dynamic_slice_in_dim(page_table, replica_idx * sessions, sessions, 0)
    my_column = lax.dynamic_slice_in_dim(table_rows, tensor_idx, 1, 1)[:, 0]
    page_index = jnp.take(my_column, from_here.reshape(-1), axis=0)
    chosen = jnp.take(kv_pool, page_index, axis=0).reshape(replicas, SHARE, PAGE, KVH, pair_width)
    outgoing = jnp.take(chosen, owner_head, axis=3)
    outgoing = jnp.transpose(outgoing, (0, 3, 1, 2, 4)).reshape(
        replicas * tensors, SHARE, PAGE, pair_width
    )
    arrived = lax.all_to_all(
        outgoing, ("replica", "tensor"), split_axis=0, concat_axis=0, tiled=True
    )
    arrived = arrived.reshape(replicas, tensors, SHARE, PAGE, pair_width)
    prefix_blocks = jnp.transpose(arrived, (0, 2, 1, 3, 4)).reshape(
        sessions, cached_len, pair_width
    )
    kv_group = tensor_idx * heads_local // GROUP
    fresh_pair = lax.dynamic_slice_in_dim(new_kv, kv_group * pair_width, pair_width, 1)
    rows_here = queries.shape[0]
    slot_rows = ROWS // 4
    query_heads = queries.reshape(rows_here, heads_local, HD)
    counts = lax.dynamic_slice_in_dim(turn_rows, replica_idx, 1, 0)[0]
    bounds = jnp.cumsum(counts, dtype=jnp.int32)
    starts = bounds - counts
    row_ids = jnp.arange(rows_here, dtype=jnp.int32)
    row_slot = jnp.sum(
        (row_ids[:, None] >= bounds[None, :]).astype(jnp.int32), axis=1, dtype=jnp.int32
    )
    offsets = jnp.arange(slot_rows, dtype=jnp.int32)
    padded_index = jnp.minimum(starts[:, None] + offsets[None, :], rows_here - 1).reshape(-1)
    slot_queries = jnp.take(query_heads, padded_index, axis=0).reshape(
        sessions, slot_rows, heads_local, HD
    )
    slot_fresh = jnp.take(fresh_pair, padded_index, axis=0).reshape(sessions, slot_rows, pair_width)
    lengths = lax.dynamic_slice_in_dim(prefix_len, replica_idx * sessions, sessions, 0)
    key_pos = jnp.arange(cached_len, dtype=jnp.int32)
    prefix_mask = (key_pos[None, :] < lengths[:, None])[:, None, :]
    fresh_mask = (offsets[None, None, :] <= offsets[None, :, None]) & (
        offsets[None, None, :] < counts[:, None, None]
    )
    score_scale = HD ** (-0.5)
    prefix_scores = (
        jnp.einsum(
            "smhd,skd->hsmk",
            slot_queries,
            prefix_blocks[:, :, :HD],
            preferred_element_type=jnp.float32,
        )
        * score_scale
    )
    fresh_scores = (
        jnp.einsum(
            "smhd,snd->hsmn",
            slot_queries,
            slot_fresh[:, :, :HD],
            preferred_element_type=jnp.float32,
        )
        * score_scale
    )
    prefix_scores = jnp.where(prefix_mask[None], prefix_scores, -jnp.inf)
    fresh_scores = jnp.where(fresh_mask[None], fresh_scores, -jnp.inf)
    row_peak = jnp.maximum(jnp.max(prefix_scores, axis=3), jnp.max(fresh_scores, axis=3))
    prefix_weights = jnp.exp(prefix_scores - row_peak[..., None])
    fresh_weights = jnp.exp(fresh_scores - row_peak[..., None])
    denominator = jnp.sum(prefix_weights, axis=3) + jnp.sum(fresh_weights, axis=3)
    mixed_values = jnp.einsum(
        "hsmk,skd->smhd",
        prefix_weights.astype(jnp.bfloat16),
        prefix_blocks[:, :, HD:],
        preferred_element_type=jnp.float32,
    )
    mixed_values = mixed_values + jnp.einsum(
        "hsmn,snd->smhd",
        fresh_weights.astype(jnp.bfloat16),
        slot_fresh[:, :, HD:],
        preferred_element_type=jnp.float32,
    )
    slot_attended = (mixed_values / jnp.transpose(denominator, (1, 2, 0))[..., None]).astype(
        jnp.bfloat16
    )
    slot_attended = slot_attended.reshape(sessions * slot_rows, heads_local * HD)
    back_index = row_slot * slot_rows + row_ids - jnp.take(starts, row_slot, axis=0)
    attended = jnp.take(slot_attended, back_index, axis=0)
    partial_out = jnp.dot(
        lax.all_gather(attended, "replica", axis=0, tiled=True),
        out_weight,
        preferred_element_type=jnp.float32,
    )
    all_rows = partial_out.shape[0]
    width = partial_out.shape[1]
    part_rows = all_rows // tensors
    head_parts = lax.all_to_all(
        partial_out.astype(jnp.bfloat16).reshape(tensors, part_rows, width),
        "tensor",
        split_axis=0,
        concat_axis=0,
        tiled=True,
    )
    head_sum = jnp.sum(head_parts.astype(jnp.float32), axis=0)
    my_residual = lax.dynamic_slice_in_dim(residual, tensor_idx * part_rows, part_rows, 0)
    carried = my_residual.astype(jnp.float32) + head_sum
    gain_row = norm_gain.astype(jnp.float32)
    squares = lax.psum(jnp.sum(carried * carried, axis=1), "replica")
    normed_part = (
        carried * lax.rsqrt(squares / D + EPSILON)[:, None] * gain_row[None, :]
    ).astype(jnp.bfloat16)
    normed = lax.all_gather(normed_part, "tensor", axis=0, tiled=True)
    weights_local = gate_up.reshape(gate_up.shape[0], 2 * gate_up.shape[2])
    slab = jnp.dot(normed, weights_local, preferred_element_type=jnp.float32)
    slab_parts = lax.all_to_all(
        slab.astype(jnp.bfloat16).reshape(replicas, rows_here, slab.shape[1]),
        "replica",
        split_axis=0,
        concat_axis=0,
        tiled=True,
    )
    summed = jnp.sum(slab_parts.astype(jnp.float32), axis=0)
    paired = summed.reshape(rows_here, 2, gate_up.shape[2])
    return (jax.nn.silu(paired[:, 0, :]) * paired[:, 1, :]).astype(jnp.bfloat16)


def solution(mesh):
    placed = (
        P("replica", "tensor"),
        P("replica", None),
        P(("replica", "tensor"), None, None),
        P(),
        P(),
        P(),
        P(),
        P("tensor", "replica"),
        P(None, "replica"),
        P("replica"),
        P("replica", None, "tensor"),
    )
    return jax.shard_map(
        per_device, mesh=mesh, in_specs=placed, out_specs=P("replica", "tensor"), check_vma=False
    )
```

```python
import jax
import jax.numpy as jnp
import numpy as np
from jax import lax
from jax.sharding import PartitionSpec as P

D = 16384
HD = 128
HEADS = 64
KVH = 4
PAGE = 64
SHARE = 1
ROWS = 128
GROUP = 16


EPSILON = 1e-05


def per_device(
    queries,
    new_kv,
    kv_pool,
    anchor,
    page_table,
    prefix_len,
    turn_rows,
    out_weight,
    residual,
    norm_gain,
    gate_up,
):
    replicas = lax.axis_size("replica")
    tensors = lax.axis_size("tensor")
    replica_idx = lax.axis_index("replica")
    tensor_idx = lax.axis_index("tensor")
    sessions = SHARE * replicas
    heads_local = HEADS // tensors
    pair_width = 2 * HD
    cached_len = tensors * PAGE
    owner_head = np.arange(tensors) * heads_local // GROUP
    from_here = lax.dynamic_slice_in_dim(anchor, replica_idx * SHARE, SHARE, 1)
    table_rows = lax.dynamic_slice_in_dim(page_table, replica_idx * sessions, sessions, 0)
    my_column = lax.dynamic_slice_in_dim(table_rows, tensor_idx, 1, 1)[:, 0]
    page_index = jnp.take(my_column, from_here.reshape(-1), axis=0)
    chosen = jnp.take(kv_pool, page_index, axis=0).reshape(replicas, SHARE, PAGE, KVH, pair_width)
    outgoing = jnp.take(chosen, owner_head, axis=3)
    outgoing = jnp.transpose(outgoing, (0, 3, 1, 2, 4)).reshape(
        replicas * tensors, SHARE, PAGE, pair_width
    )
    arrived = lax.all_to_all(
        outgoing, ("replica", "tensor"), split_axis=0, concat_axis=0, tiled=True
    )
    arrived = arrived.reshape(replicas, tensors, SHARE, PAGE, pair_width)
    prefix_blocks = jnp.transpose(arrived, (0, 2, 1, 3, 4)).reshape(
        sessions, cached_len, pair_width
    )
    kv_group = tensor_idx * heads_local // GROUP
    fresh_pair = lax.dynamic_slice_in_dim(new_kv, kv_group * pair_width, pair_width, 1)
    rows_here = queries.shape[0]
    slot_rows = ROWS // 4
    query_heads = queries.reshape(rows_here, heads_local, HD)
    counts = lax.dynamic_slice_in_dim(turn_rows, replica_idx, 1, 0)[0]
    bounds = jnp.cumsum(counts, dtype=jnp.int32)
    starts = bounds - counts
    row_ids = jnp.arange(rows_here, dtype=jnp.int32)
    row_slot = jnp.sum(
        (row_ids[:, None] >= bounds[None, :]).astype(jnp.int32), axis=1, dtype=jnp.int32
    )
    offsets = jnp.arange(slot_rows, dtype=jnp.int32)
    padded_index = jnp.minimum(starts[:, None] + offsets[None, :], rows_here - 1).reshape(-1)
    slot_queries = jnp.take(query_heads, padded_index, axis=0).reshape(
        sessions, slot_rows, heads_local, HD
    )
    slot_fresh = jnp.take(fresh_pair, padded_index, axis=0).reshape(sessions, slot_rows, pair_width)
    lengths = lax.dynamic_slice_in_dim(prefix_len, replica_idx * sessions, sessions, 0)
    key_pos = jnp.arange(cached_len, dtype=jnp.int32)
    prefix_mask = (key_pos[None, :] < lengths[:, None])[:, None, :]
    fresh_mask = (offsets[None, None, :] <= offsets[None, :, None]) & (
        offsets[None, None, :] < counts[:, None, None]
    )
    score_scale = HD ** (-0.5)
    prefix_scores = (
        jnp.einsum(
            "smhd,skd->hsmk",
            slot_queries,
            prefix_blocks[:, :, :HD],
            preferred_element_type=jnp.float32,
        )
        * score_scale
    )
    fresh_scores = (
        jnp.einsum(
            "smhd,snd->hsmn",
            slot_queries,
            slot_fresh[:, :, :HD],
            preferred_element_type=jnp.float32,
        )
        * score_scale
    )
    prefix_scores = jnp.where(prefix_mask[None], prefix_scores, -jnp.inf)
    fresh_scores = jnp.where(fresh_mask[None], fresh_scores, -jnp.inf)
    row_peak = jnp.maximum(jnp.max(prefix_scores, axis=3), jnp.max(fresh_scores, axis=3))
    prefix_weights = jnp.exp(prefix_scores - row_peak[..., None])
    fresh_weights = jnp.exp(fresh_scores - row_peak[..., None])
    denominator = jnp.sum(prefix_weights, axis=3) + jnp.sum(fresh_weights, axis=3)
    mixed_values = jnp.einsum(
        "hsmk,skd->smhd",
        prefix_weights.astype(jnp.bfloat16),
        prefix_blocks[:, :, HD:],
        preferred_element_type=jnp.float32,
    )
    mixed_values = mixed_values + jnp.einsum(
        "hsmn,snd->smhd",
        fresh_weights.astype(jnp.bfloat16),
        slot_fresh[:, :, HD:],
        preferred_element_type=jnp.float32,
    )
    slot_attended = (mixed_values / jnp.transpose(denominator, (1, 2, 0))[..., None]).astype(
        jnp.bfloat16
    )
    slot_attended = slot_attended.reshape(sessions * slot_rows, heads_local * HD)
    back_index = row_slot * slot_rows + row_ids - jnp.take(starts, row_slot, axis=0)
    attended = jnp.take(slot_attended, back_index, axis=0)
    gathered = lax.all_to_all(
        jnp.broadcast_to(attended[None], (replicas,) + attended.shape),
        "replica",
        split_axis=0,
        concat_axis=0,
        tiled=True,
    ).reshape(replicas * rows_here, attended.shape[1])
    partial_out = jnp.dot(
        gathered,
        out_weight,
        preferred_element_type=jnp.float32,
    )
    all_rows = partial_out.shape[0]
    width = partial_out.shape[1]
    part_rows = all_rows // tensors
    head_parts = lax.all_to_all(
        partial_out.astype(jnp.bfloat16).reshape(tensors, part_rows, width),
        "tensor",
        split_axis=0,
        concat_axis=0,
        tiled=True,
    )
    head_sum = jnp.sum(head_parts.astype(jnp.float32), axis=0)
    my_residual = lax.dynamic_slice_in_dim(residual, tensor_idx * part_rows, part_rows, 0)
    carried = my_residual.astype(jnp.float32) + head_sum
    gain_row = norm_gain.astype(jnp.float32)
    squares = lax.psum(jnp.sum(carried * carried, axis=1), "replica")
    normed_part = (
        carried * lax.rsqrt(squares / D + EPSILON)[:, None] * gain_row[None, :]
    ).astype(jnp.bfloat16)
    normed = lax.all_gather(normed_part, "tensor", axis=0, tiled=True)
    weights_local = gate_up.reshape(gate_up.shape[0], 2 * gate_up.shape[2])
    chunks = 2
    chunk_rows = rows_here // chunks
    normed_chunks = normed.reshape(replicas, chunks, chunk_rows, normed.shape[1])
    outs = []
    for c in range(chunks):
        slab = jnp.dot(
            normed_chunks[:, c].reshape(replicas * chunk_rows, normed.shape[1]),
            weights_local,
            preferred_element_type=jnp.float32,
        )
        slab_parts = lax.all_to_all(
            slab.astype(jnp.bfloat16).reshape(replicas, chunk_rows, slab.shape[1]),
            "replica",
            split_axis=0,
            concat_axis=0,
            tiled=True,
        )
        summed = jnp.sum(slab_parts.astype(jnp.float32), axis=0)
        paired = summed.reshape(chunk_rows, 2, gate_up.shape[2])
        outs.append((jax.nn.silu(paired[:, 0, :]) * paired[:, 1, :]).astype(jnp.bfloat16))
    return jnp.concatenate(outs, axis=0)


def solution(mesh):
    placed = (
        P("replica", "tensor"),
        P("replica", None),
        P(("replica", "tensor"), None, None),
        P(),
        P(),
        P(),
        P(),
        P("tensor", "replica"),
        P(None, "replica"),
        P("replica"),
        P("replica", None, "tensor"),
    )
    return jax.shard_map(
        per_device, mesh=mesh, in_specs=placed, out_specs=P("replica", "tensor"), check_vma=False
    )
```

```python
import jax
import jax.numpy as jnp
import numpy as np
from jax import lax
from jax.sharding import PartitionSpec as P

D = 16384
HD = 128
HEADS = 64
KVH = 4
PAGE = 64
SHARE = 1
ROWS = 128
GROUP = 16


EPSILON = 1e-05


def per_device(
    queries,
    new_kv,
    kv_pool,
    anchor,
    page_table,
    prefix_len,
    turn_rows,
    out_weight,
    residual,
    norm_gain,
    gate_up,
):
    replicas = lax.axis_size("replica")
    tensors = lax.axis_size("tensor")
    replica_idx = lax.axis_index("replica")
    tensor_idx = lax.axis_index("tensor")
    sessions = SHARE * replicas
    heads_local = HEADS // tensors
    pair_width = 2 * HD
    cached_len = tensors * PAGE
    owner_head = np.arange(tensors) * heads_local // GROUP
    from_here = lax.dynamic_slice_in_dim(anchor, replica_idx * SHARE, SHARE, 1)
    table_rows = lax.dynamic_slice_in_dim(page_table, replica_idx * sessions, sessions, 0)
    my_column = lax.dynamic_slice_in_dim(table_rows, tensor_idx, 1, 1)[:, 0]
    page_index = jnp.take(my_column, from_here.reshape(-1), axis=0)
    chosen = jnp.take(kv_pool, page_index, axis=0).reshape(replicas, SHARE, PAGE, KVH, pair_width)
    outgoing = jnp.take(chosen, owner_head, axis=3)
    outgoing = jnp.transpose(outgoing, (0, 3, 1, 2, 4)).reshape(
        replicas * tensors, SHARE, PAGE, pair_width
    )
    arrived = lax.all_to_all(
        outgoing, ("replica", "tensor"), split_axis=0, concat_axis=0, tiled=True
    )
    arrived = arrived.reshape(replicas, tensors, SHARE, PAGE, pair_width)
    prefix_blocks = jnp.transpose(arrived, (0, 2, 1, 3, 4)).reshape(
        sessions, cached_len, pair_width
    )
    kv_group = tensor_idx * heads_local // GROUP
    fresh_pair = lax.dynamic_slice_in_dim(new_kv, kv_group * pair_width, pair_width, 1)
    rows_here = queries.shape[0]
    slot_rows = ROWS // 4
    query_heads = queries.reshape(rows_here, heads_local, HD)
    counts = lax.dynamic_slice_in_dim(turn_rows, replica_idx, 1, 0)[0]
    bounds = jnp.cumsum(counts, dtype=jnp.int32)
    starts = bounds - counts
    row_ids = jnp.arange(rows_here, dtype=jnp.int32)
    row_slot = jnp.sum(
        (row_ids[:, None] >= bounds[None, :]).astype(jnp.int32), axis=1, dtype=jnp.int32
    )
    offsets = jnp.arange(slot_rows, dtype=jnp.int32)
    padded_index = jnp.minimum(starts[:, None] + offsets[None, :], rows_here - 1).reshape(-1)
    slot_queries = jnp.take(query_heads, padded_index, axis=0).reshape(
        sessions, slot_rows, heads_local, HD
    )
    slot_fresh = jnp.take(fresh_pair, padded_index, axis=0).reshape(sessions, slot_rows, pair_width)
    lengths = lax.dynamic_slice_in_dim(prefix_len, replica_idx * sessions, sessions, 0)
    key_pos = jnp.arange(cached_len, dtype=jnp.int32)
    prefix_mask = (key_pos[None, :] < lengths[:, None])[:, None, :]
    fresh_mask = (offsets[None, None, :] <= offsets[None, :, None]) & (
        offsets[None, None, :] < counts[:, None, None]
    )
    score_scale = HD ** (-0.5)
    prefix_scores = (
        jnp.einsum(
            "smhd,skd->hsmk",
            slot_queries,
            prefix_blocks[:, :, :HD],
            preferred_element_type=jnp.float32,
        )
        * score_scale
    )
    fresh_scores = (
        jnp.einsum(
            "smhd,snd->hsmn",
            slot_queries,
            slot_fresh[:, :, :HD],
            preferred_element_type=jnp.float32,
        )
        * score_scale
    )
    prefix_scores = jnp.where(prefix_mask[None], prefix_scores, -jnp.inf)
    fresh_scores = jnp.where(fresh_mask[None], fresh_scores, -jnp.inf)
    row_peak = jnp.maximum(jnp.max(prefix_scores, axis=3), jnp.max(fresh_scores, axis=3))
    prefix_weights = jnp.exp(prefix_scores - row_peak[..., None])
    fresh_weights = jnp.exp(fresh_scores - row_peak[..., None])
    denominator = jnp.sum(prefix_weights, axis=3) + jnp.sum(fresh_weights, axis=3)
    mixed_values = jnp.einsum(
        "hsmk,skd->smhd",
        prefix_weights.astype(jnp.bfloat16),
        prefix_blocks[:, :, HD:],
        preferred_element_type=jnp.float32,
    )
    mixed_values = mixed_values + jnp.einsum(
        "hsmn,snd->smhd",
        fresh_weights.astype(jnp.bfloat16),
        slot_fresh[:, :, HD:],
        preferred_element_type=jnp.float32,
    )
    slot_attended = (mixed_values / jnp.transpose(denominator, (1, 2, 0))[..., None]).astype(
        jnp.bfloat16
    )
    slot_attended = slot_attended.reshape(sessions * slot_rows, heads_local * HD)
    back_index = row_slot * slot_rows + row_ids - jnp.take(starts, row_slot, axis=0)
    attended = jnp.take(slot_attended, back_index, axis=0)
    gathered = lax.all_to_all(
        jnp.broadcast_to(attended[None], (replicas,) + attended.shape),
        "replica",
        split_axis=0,
        concat_axis=0,
        tiled=True,
    ).reshape(replicas * rows_here, attended.shape[1])
    partial_out = jnp.dot(
        gathered,
        out_weight,
        preferred_element_type=jnp.float32,
    )
    all_rows = partial_out.shape[0]
    width = partial_out.shape[1]
    part_rows = all_rows // tensors
    head_parts = lax.all_to_all(
        partial_out.astype(jnp.bfloat16).reshape(tensors, part_rows, width),
        "tensor",
        split_axis=0,
        concat_axis=0,
        tiled=True,
    )
    head_sum = jnp.sum(head_parts.astype(jnp.float32), axis=0)
    my_residual = lax.dynamic_slice_in_dim(residual, tensor_idx * part_rows, part_rows, 0)
    carried = my_residual.astype(jnp.float32) + head_sum
    gain_row = norm_gain.astype(jnp.float32)
    lane = 128
    part_squares = jnp.sum(carried * carried, axis=1)
    square_hi = part_squares.astype(jnp.bfloat16)
    square_lo = (part_squares - square_hi.astype(jnp.float32)).astype(jnp.bfloat16)
    square_block = jnp.zeros((part_rows, lane), jnp.bfloat16)
    square_block = square_block.at[:, 0].set(square_hi).at[:, 1].set(square_lo)
    scaled = (carried * gain_row[None, :]).astype(jnp.bfloat16)
    gathered_rows = lax.all_gather(
        jnp.concatenate([scaled, square_block], axis=1), "tensor", axis=0, tiled=True
    )
    normed = gathered_rows[:, :width]
    row_squares = gathered_rows[:, width].astype(jnp.float32) + gathered_rows[
        :, width + 1
    ].astype(jnp.float32)
    weights_local = gate_up.reshape(gate_up.shape[0], 2 * gate_up.shape[2])
    slab = jnp.dot(normed, weights_local, preferred_element_type=jnp.float32)
    slab_cols = slab.shape[1]
    row_hi = row_squares.astype(jnp.bfloat16)
    row_lo = (row_squares - row_hi.astype(jnp.float32)).astype(jnp.bfloat16)
    row_block = jnp.zeros((slab.shape[0], lane), jnp.bfloat16)
    row_block = row_block.at[:, 0].set(row_hi).at[:, 1].set(row_lo)
    payload = jnp.concatenate([slab.astype(jnp.bfloat16), row_block], axis=1)
    slab_parts = lax.all_to_all(
        payload.reshape(replicas, rows_here, slab_cols + lane),
        "replica",
        split_axis=0,
        concat_axis=0,
        tiled=True,
    )
    summed = jnp.sum(slab_parts.astype(jnp.float32), axis=0)
    total_squares = summed[:, slab_cols] + summed[:, slab_cols + 1]
    inv_rms = lax.rsqrt(total_squares / D + EPSILON)
    paired = summed[:, :slab_cols].reshape(rows_here, 2, gate_up.shape[2])
    gate = paired[:, 0, :] * inv_rms[:, None]
    up = paired[:, 1, :] * inv_rms[:, None]
    return (jax.nn.silu(gate) * up).astype(jnp.bfloat16)


def solution(mesh):
    placed = (
        P("replica", "tensor"),
        P("replica", None),
        P(("replica", "tensor"), None, None),
        P(),
        P(),
        P(),
        P(),
        P("tensor", "replica"),
        P(None, "replica"),
        P("replica"),
        P("replica", None, "tensor"),
    )
    return jax.shard_map(
        per_device, mesh=mesh, in_specs=placed, out_specs=P("replica", "tensor"), check_vma=False
    )
```

```python
import jax
import jax.numpy as jnp
import numpy as np
from jax import lax
from jax.sharding import PartitionSpec as P

D = 16384
HD = 128
HEADS = 64
KVH = 4
PAGE = 64
SHARE = 1
ROWS = 128
GROUP = 16


EPSILON = 1e-05


def per_device(
    queries,
    new_kv,
    kv_pool,
    anchor,
    page_table,
    prefix_len,
    turn_rows,
    out_weight,
    residual,
    norm_gain,
    gate_up,
):
    replicas = lax.axis_size("replica")
    tensors = lax.axis_size("tensor")
    replica_idx = lax.axis_index("replica")
    tensor_idx = lax.axis_index("tensor")
    sessions = SHARE * replicas
    heads_local = HEADS // tensors
    pair_width = 2 * HD
    cached_len = tensors * PAGE
    owner_head = np.arange(tensors) * heads_local // GROUP
    from_here = lax.dynamic_slice_in_dim(anchor, replica_idx * SHARE, SHARE, 1)
    table_rows = lax.dynamic_slice_in_dim(page_table, replica_idx * sessions, sessions, 0)
    my_column = lax.dynamic_slice_in_dim(table_rows, tensor_idx, 1, 1)[:, 0]
    page_index = jnp.take(my_column, from_here.reshape(-1), axis=0)
    chosen = jnp.take(kv_pool, page_index, axis=0).reshape(replicas, SHARE, PAGE, KVH, pair_width)
    half = PAGE // 2
    core_half = np.arange(tensors) % 2
    outgoing = jnp.take(chosen, owner_head, axis=3)
    outgoing = outgoing.reshape(replicas, SHARE, 2, half, tensors, pair_width)
    outgoing = outgoing[:, :, core_half, :, np.arange(tensors), :]
    outgoing = jnp.transpose(outgoing, (1, 0, 2, 3, 4)).reshape(
        replicas * tensors, SHARE, half, pair_width
    )
    arrived = lax.all_to_all(
        outgoing, ("replica", "tensor"), split_axis=0, concat_axis=0, tiled=True
    )
    partner = lax.ppermute(arrived, "tensor", [(i, i ^ 1) for i in range(tensors)])
    mine_first = (tensor_idx % 2) == 0
    low_half = jnp.where(mine_first, arrived, partner)
    high_half = jnp.where(mine_first, partner, arrived)
    arrived = jnp.concatenate([low_half, high_half], axis=2)
    arrived = arrived.reshape(replicas, tensors, SHARE, PAGE, pair_width)
    prefix_blocks = jnp.transpose(arrived, (0, 2, 1, 3, 4)).reshape(
        sessions, cached_len, pair_width
    )
    kv_group = tensor_idx * heads_local // GROUP
    fresh_pair = lax.dynamic_slice_in_dim(new_kv, kv_group * pair_width, pair_width, 1)
    rows_here = queries.shape[0]
    slot_rows = ROWS // 4
    query_heads = queries.reshape(rows_here, heads_local, HD)
    counts = lax.dynamic_slice_in_dim(turn_rows, replica_idx, 1, 0)[0]
    bounds = jnp.cumsum(counts, dtype=jnp.int32)
    starts = bounds - counts
    row_ids = jnp.arange(rows_here, dtype=jnp.int32)
    row_slot = jnp.sum(
        (row_ids[:, None] >= bounds[None, :]).astype(jnp.int32), axis=1, dtype=jnp.int32
    )
    offsets = jnp.arange(slot_rows, dtype=jnp.int32)
    padded_index = jnp.minimum(starts[:, None] + offsets[None, :], rows_here - 1).reshape(-1)
    slot_queries = jnp.take(query_heads, padded_index, axis=0).reshape(
        sessions, slot_rows, heads_local, HD
    )
    slot_fresh = jnp.take(fresh_pair, padded_index, axis=0).reshape(sessions, slot_rows, pair_width)
    lengths = lax.dynamic_slice_in_dim(prefix_len, replica_idx * sessions, sessions, 0)
    key_pos = jnp.arange(cached_len, dtype=jnp.int32)
    prefix_mask = (key_pos[None, :] < lengths[:, None])[:, None, :]
    fresh_mask = (offsets[None, None, :] <= offsets[None, :, None]) & (
        offsets[None, None, :] < counts[:, None, None]
    )
    score_scale = HD ** (-0.5)
    prefix_scores = (
        jnp.einsum(
            "smhd,skd->hsmk",
            slot_queries,
            prefix_blocks[:, :, :HD],
            preferred_element_type=jnp.float32,
        )
        * score_scale
    )
    fresh_scores = (
        jnp.einsum(
            "smhd,snd->hsmn",
            slot_queries,
            slot_fresh[:, :, :HD],
            preferred_element_type=jnp.float32,
        )
        * score_scale
    )
    prefix_scores = jnp.where(prefix_mask[None], prefix_scores, -jnp.inf)
    fresh_scores = jnp.where(fresh_mask[None], fresh_scores, -jnp.inf)
    row_peak = jnp.maximum(jnp.max(prefix_scores, axis=3), jnp.max(fresh_scores, axis=3))
    prefix_weights = jnp.exp(prefix_scores - row_peak[..., None])
    fresh_weights = jnp.exp(fresh_scores - row_peak[..., None])
    denominator = jnp.sum(prefix_weights, axis=3) + jnp.sum(fresh_weights, axis=3)
    mixed_values = jnp.einsum(
        "hsmk,skd->smhd",
        prefix_weights.astype(jnp.bfloat16),
        prefix_blocks[:, :, HD:],
        preferred_element_type=jnp.float32,
    )
    mixed_values = mixed_values + jnp.einsum(
        "hsmn,snd->smhd",
        fresh_weights.astype(jnp.bfloat16),
        slot_fresh[:, :, HD:],
        preferred_element_type=jnp.float32,
    )
    slot_attended = (mixed_values / jnp.transpose(denominator, (1, 2, 0))[..., None]).astype(
        jnp.bfloat16
    )
    slot_attended = slot_attended.reshape(sessions * slot_rows, heads_local * HD)
    back_index = row_slot * slot_rows + row_ids - jnp.take(starts, row_slot, axis=0)
    attended = jnp.take(slot_attended, back_index, axis=0)
    gathered = lax.all_to_all(
        jnp.broadcast_to(attended[None], (replicas,) + attended.shape),
        "replica",
        split_axis=0,
        concat_axis=0,
        tiled=True,
    ).reshape(replicas * rows_here, attended.shape[1])
    partial_out = jnp.dot(
        gathered,
        out_weight,
        preferred_element_type=jnp.float32,
    )
    all_rows = partial_out.shape[0]
    width = partial_out.shape[1]
    part_rows = all_rows // tensors
    head_parts = lax.all_to_all(
        partial_out.astype(jnp.bfloat16).reshape(tensors, part_rows, width),
        "tensor",
        split_axis=0,
        concat_axis=0,
        tiled=True,
    )
    head_sum = jnp.sum(head_parts.astype(jnp.float32), axis=0)
    my_residual = lax.dynamic_slice_in_dim(residual, tensor_idx * part_rows, part_rows, 0)
    carried = my_residual.astype(jnp.float32) + head_sum
    gain_row = norm_gain.astype(jnp.float32)
    squares = jnp.sum(carried * carried, axis=1)
    step = 1
    while step < replicas:
        squares = squares + lax.ppermute(
            squares, "replica", [(i, i ^ step) for i in range(replicas)]
        )
        step *= 2
    normed_part = (
        carried * lax.rsqrt(squares / D + EPSILON)[:, None] * gain_row[None, :]
    ).astype(jnp.bfloat16)
    normed = lax.all_gather(normed_part, "tensor", axis=0, tiled=True)
    weights_local = gate_up.reshape(gate_up.shape[0], 2 * gate_up.shape[2])
    slab = jnp.dot(normed, weights_local, preferred_element_type=jnp.float32)
    slab_parts = lax.all_to_all(
        slab.astype(jnp.bfloat16).reshape(replicas, rows_here, slab.shape[1]),
        "replica",
        split_axis=0,
        concat_axis=0,
        tiled=True,
    )
    summed = jnp.sum(slab_parts.astype(jnp.float32), axis=0)
    paired = summed.reshape(rows_here, 2, gate_up.shape[2])
    return (jax.nn.silu(paired[:, 0, :]) * paired[:, 1, :]).astype(jnp.bfloat16)


def solution(mesh):
    placed = (
        P("replica", "tensor"),
        P("replica", None),
        P(("replica", "tensor"), None, None),
        P(),
        P(),
        P(),
        P(),
        P("tensor", "replica"),
        P(None, "replica"),
        P("replica"),
        P("replica", None, "tensor"),
    )
    return jax.shard_map(
        per_device, mesh=mesh, in_specs=placed, out_specs=P("replica", "tensor"), check_vma=False
    )
```

```python
import jax
import jax.numpy as jnp
import numpy as np
from jax import lax
from jax.sharding import PartitionSpec as P

D = 16384
HD = 128
HEADS = 64
KVH = 4
PAGE = 64
SHARE = 1
ROWS = 128
GROUP = 16


EPSILON = 1e-05


def per_device(
    queries,
    new_kv,
    kv_pool,
    anchor,
    page_table,
    prefix_len,
    turn_rows,
    out_weight,
    residual,
    norm_gain,
    gate_up,
):
    replicas = lax.axis_size(("zh", "y"))
    tensors = lax.axis_size(("x", "zl", "core"))
    replica_idx = lax.axis_index(("zh", "y"))
    tensor_idx = lax.axis_index(("x", "zl", "core"))
    sessions = SHARE * replicas
    heads_local = HEADS // tensors
    pair_width = 2 * HD
    cached_len = tensors * PAGE
    owner_head = np.arange(tensors) * heads_local // GROUP
    from_here = lax.dynamic_slice_in_dim(anchor, replica_idx * SHARE, SHARE, 1)
    table_rows = lax.dynamic_slice_in_dim(page_table, replica_idx * sessions, sessions, 0)
    my_column = lax.dynamic_slice_in_dim(table_rows, tensor_idx, 1, 1)[:, 0]
    page_index = jnp.take(my_column, from_here.reshape(-1), axis=0)
    chosen = jnp.take(kv_pool, page_index, axis=0).reshape(replicas, SHARE, PAGE, KVH, pair_width)
    half = PAGE // 2
    core_half = np.arange(tensors) % 2
    outgoing = jnp.take(chosen, owner_head, axis=3)
    outgoing = outgoing.reshape(replicas, SHARE, 2, half, tensors, pair_width)
    outgoing = outgoing[:, :, core_half, :, np.arange(tensors), :]
    outgoing = jnp.transpose(outgoing, (1, 0, 2, 3, 4)).reshape(
        replicas * tensors, SHARE, half, pair_width
    )
    arrived = lax.all_to_all(
        outgoing, ("zh", "y", "x", "zl", "core"), split_axis=0, concat_axis=0, tiled=True
    )
    partner = lax.ppermute(arrived, ("x", "zl", "core"), [(i, i ^ 1) for i in range(tensors)])
    mine_first = (tensor_idx % 2) == 0
    low_half = jnp.where(mine_first, arrived, partner)
    high_half = jnp.where(mine_first, partner, arrived)
    arrived = jnp.concatenate([low_half, high_half], axis=2)
    arrived = arrived.reshape(replicas, tensors, SHARE, PAGE, pair_width)
    prefix_blocks = jnp.transpose(arrived, (0, 2, 1, 3, 4)).reshape(
        sessions, cached_len, pair_width
    )
    kv_group = tensor_idx * heads_local // GROUP
    fresh_pair = lax.dynamic_slice_in_dim(new_kv, kv_group * pair_width, pair_width, 1)
    rows_here = queries.shape[0]
    slot_rows = ROWS // 4
    query_heads = queries.reshape(rows_here, heads_local, HD)
    counts = lax.dynamic_slice_in_dim(turn_rows, replica_idx, 1, 0)[0]
    bounds = jnp.cumsum(counts, dtype=jnp.int32)
    starts = bounds - counts
    row_ids = jnp.arange(rows_here, dtype=jnp.int32)
    row_slot = jnp.sum(
        (row_ids[:, None] >= bounds[None, :]).astype(jnp.int32), axis=1, dtype=jnp.int32
    )
    offsets = jnp.arange(slot_rows, dtype=jnp.int32)
    padded_index = jnp.minimum(starts[:, None] + offsets[None, :], rows_here - 1).reshape(-1)
    slot_queries = jnp.take(query_heads, padded_index, axis=0).reshape(
        sessions, slot_rows, heads_local, HD
    )
    slot_fresh = jnp.take(fresh_pair, padded_index, axis=0).reshape(sessions, slot_rows, pair_width)
    lengths = lax.dynamic_slice_in_dim(prefix_len, replica_idx * sessions, sessions, 0)
    key_pos = jnp.arange(cached_len, dtype=jnp.int32)
    prefix_mask = (key_pos[None, :] < lengths[:, None])[:, None, :]
    fresh_mask = (offsets[None, None, :] <= offsets[None, :, None]) & (
        offsets[None, None, :] < counts[:, None, None]
    )
    score_scale = HD ** (-0.5)
    prefix_scores = (
        jnp.einsum(
            "smhd,skd->hsmk",
            slot_queries,
            prefix_blocks[:, :, :HD],
            preferred_element_type=jnp.float32,
        )
        * score_scale
    )
    fresh_scores = (
        jnp.einsum(
            "smhd,snd->hsmn",
            slot_queries,
            slot_fresh[:, :, :HD],
            preferred_element_type=jnp.float32,
        )
        * score_scale
    )
    prefix_scores = jnp.where(prefix_mask[None], prefix_scores, -jnp.inf)
    fresh_scores = jnp.where(fresh_mask[None], fresh_scores, -jnp.inf)
    row_peak = jnp.maximum(jnp.max(prefix_scores, axis=3), jnp.max(fresh_scores, axis=3))
    prefix_weights = jnp.exp(prefix_scores - row_peak[..., None])
    fresh_weights = jnp.exp(fresh_scores - row_peak[..., None])
    denominator = jnp.sum(prefix_weights, axis=3) + jnp.sum(fresh_weights, axis=3)
    mixed_values = jnp.einsum(
        "hsmk,skd->smhd",
        prefix_weights.astype(jnp.bfloat16),
        prefix_blocks[:, :, HD:],
        preferred_element_type=jnp.float32,
    )
    mixed_values = mixed_values + jnp.einsum(
        "hsmn,snd->smhd",
        fresh_weights.astype(jnp.bfloat16),
        slot_fresh[:, :, HD:],
        preferred_element_type=jnp.float32,
    )
    slot_attended = (mixed_values / jnp.transpose(denominator, (1, 2, 0))[..., None]).astype(
        jnp.bfloat16
    )
    slot_attended = slot_attended.reshape(sessions * slot_rows, heads_local * HD)
    back_index = row_slot * slot_rows + row_ids - jnp.take(starts, row_slot, axis=0)
    attended = jnp.take(slot_attended, back_index, axis=0)
    gathered = lax.all_to_all(
        jnp.broadcast_to(attended[None], (replicas,) + attended.shape),
        ("zh", "y"),
        split_axis=0,
        concat_axis=0,
        tiled=True,
    ).reshape(replicas * rows_here, attended.shape[1])
    partial_out = jnp.dot(
        gathered,
        out_weight,
        preferred_element_type=jnp.float32,
    )
    all_rows = partial_out.shape[0]
    width = partial_out.shape[1]
    part_rows = all_rows // tensors
    head_parts = lax.all_to_all(
        partial_out.astype(jnp.bfloat16).reshape(tensors, part_rows, width),
        ("x", "zl", "core"),
        split_axis=0,
        concat_axis=0,
        tiled=True,
    )
    head_sum = jnp.sum(head_parts.astype(jnp.float32), axis=0)
    my_residual = lax.dynamic_slice_in_dim(residual, tensor_idx * part_rows, part_rows, 0)
    carried = my_residual.astype(jnp.float32) + head_sum
    gain_row = norm_gain.astype(jnp.float32)
    squares = jnp.sum(carried * carried, axis=1)
    step = 1
    while step < replicas:
        squares = squares + lax.ppermute(
            squares, ("zh", "y"), [(i, i ^ step) for i in range(replicas)]
        )
        step *= 2
    normed_part = (
        carried * lax.rsqrt(squares / D + EPSILON)[:, None] * gain_row[None, :]
    ).astype(jnp.bfloat16)
    normed = lax.all_gather(normed_part, ("x", "zl", "core"), axis=0, tiled=True)
    weights_local = gate_up.reshape(gate_up.shape[0], 2 * gate_up.shape[2])
    slab = jnp.dot(normed, weights_local, preferred_element_type=jnp.float32)
    slab_cols = slab.shape[1]
    high = lax.axis_size("zh")
    ring = lax.axis_size("y")
    high_idx = lax.axis_index("zh")
    by_ring = jnp.transpose(
        slab.reshape(high, ring, rows_here, slab_cols), (1, 0, 2, 3)
    ).astype(jnp.bfloat16)
    ring_parts = lax.all_to_all(by_ring, "y", split_axis=0, concat_axis=0, tiled=True)
    ring_sum = jnp.sum(ring_parts.astype(jnp.float32), axis=0)
    keep = lax.dynamic_index_in_dim(ring_sum, high_idx, 0, keepdims=False)
    give = lax.dynamic_index_in_dim(ring_sum, 1 - high_idx, 0, keepdims=False)
    give_hi = give.astype(jnp.bfloat16)
    give_lo = (give - give_hi.astype(jnp.float32)).astype(jnp.bfloat16)
    got = lax.ppermute(
        jnp.stack([give_hi, give_lo]), "zh", [(i, i ^ 1) for i in range(high)]
    ).astype(jnp.float32)
    summed = keep + got[0] + got[1]
    paired = summed.reshape(rows_here, 2, gate_up.shape[2])
    return (jax.nn.silu(paired[:, 0, :]) * paired[:, 1, :]).astype(jnp.bfloat16)


def solution(mesh):
    fine = jax.sharding.Mesh(
        mesh.devices.reshape(2, 4, 4, 2, 2), ("zh", "y", "x", "zl", "core")
    )
    rep = ("zh", "y")
    ten = ("x", "zl", "core")

    def body(*args):
        return per_device(*args)

    placed = (
        P(rep, ten),
        P(rep, None),
        P(rep + ten, None, None),
        P(),
        P(),
        P(),
        P(),
        P(ten, rep),
        P(None, rep),
        P(rep),
        P(rep, None, ten),
    )
    return jax.shard_map(
        body, mesh=fine, in_specs=placed, out_specs=P(rep, ten), check_vma=False
    )
```

```python
import jax
import jax.numpy as jnp
import numpy as np
from jax import lax
from jax.sharding import PartitionSpec as P

D = 16384
HD = 128
HEADS = 64
KVH = 4
PAGE = 64
SHARE = 1
ROWS = 128
GROUP = 16


EPSILON = 1e-05


def per_device(
    queries,
    new_kv,
    kv_pool,
    anchor,
    page_table,
    prefix_len,
    turn_rows,
    out_weight,
    residual,
    norm_gain,
    gate_up,
):
    replicas = lax.axis_size("replica")
    tensors = lax.axis_size("tensor")
    replica_idx = lax.axis_index("replica")
    tensor_idx = lax.axis_index("tensor")
    sessions = SHARE * replicas
    heads_local = HEADS // tensors
    pair_width = 2 * HD
    cached_len = tensors * PAGE
    owner_head = np.arange(tensors) * heads_local // GROUP
    from_here = lax.dynamic_slice_in_dim(anchor, replica_idx * SHARE, SHARE, 1)
    table_rows = lax.dynamic_slice_in_dim(page_table, replica_idx * sessions, sessions, 0)
    my_column = lax.dynamic_slice_in_dim(table_rows, tensor_idx, 1, 1)[:, 0]
    page_index = jnp.take(my_column, from_here.reshape(-1), axis=0)
    chosen = jnp.take(kv_pool, page_index, axis=0).reshape(replicas, SHARE, PAGE, KVH, pair_width)
    half = PAGE // 2
    lanes_per_head = tensors // KVH
    outgoing = jnp.transpose(
        chosen.reshape(replicas, 2, half, KVH, pair_width), (0, 3, 1, 2, 4)
    )
    outgoing = jnp.broadcast_to(
        outgoing[:, :, None],
        (replicas, KVH, lanes_per_head // 2, 2, half, pair_width),
    ).reshape(replicas * tensors, SHARE, half, pair_width)
    arrived = lax.all_to_all(
        outgoing, ("replica", "tensor"), split_axis=0, concat_axis=0, tiled=True
    )
    partner = lax.ppermute(arrived, "tensor", [(i, i ^ 1) for i in range(tensors)])
    mine_first = (tensor_idx % 2) == 0
    low_half = jnp.where(mine_first, arrived, partner)
    high_half = jnp.where(mine_first, partner, arrived)
    arrived = jnp.concatenate([low_half, high_half], axis=2)
    arrived = arrived.reshape(replicas, tensors, SHARE, PAGE, pair_width)
    prefix_blocks = jnp.transpose(arrived, (0, 2, 1, 3, 4)).reshape(
        sessions, cached_len, pair_width
    )
    kv_group = tensor_idx * heads_local // GROUP
    fresh_pair = lax.dynamic_slice_in_dim(new_kv, kv_group * pair_width, pair_width, 1)
    rows_here = queries.shape[0]
    slot_rows = ROWS // 4
    query_heads = queries.reshape(rows_here, heads_local, HD)
    counts = lax.dynamic_slice_in_dim(turn_rows, replica_idx, 1, 0)[0]
    bounds = jnp.cumsum(counts, dtype=jnp.int32)
    starts = bounds - counts
    row_ids = jnp.arange(rows_here, dtype=jnp.int32)
    row_slot = jnp.sum(
        (row_ids[:, None] >= bounds[None, :]).astype(jnp.int32), axis=1, dtype=jnp.int32
    )
    offsets = jnp.arange(slot_rows, dtype=jnp.int32)
    padded_index = jnp.minimum(starts[:, None] + offsets[None, :], rows_here - 1).reshape(-1)
    slot_queries = jnp.take(query_heads, padded_index, axis=0).reshape(
        sessions, slot_rows, heads_local, HD
    )
    slot_fresh = jnp.take(fresh_pair, padded_index, axis=0).reshape(sessions, slot_rows, pair_width)
    lengths = lax.dynamic_slice_in_dim(prefix_len, replica_idx * sessions, sessions, 0)
    key_pos = jnp.arange(cached_len, dtype=jnp.int32)
    prefix_mask = (key_pos[None, :] < lengths[:, None])[:, None, :]
    fresh_mask = (offsets[None, None, :] <= offsets[None, :, None]) & (
        offsets[None, None, :] < counts[:, None, None]
    )
    score_scale = HD ** (-0.5)
    prefix_scores = (
        jnp.einsum(
            "smhd,skd->hsmk",
            slot_queries,
            prefix_blocks[:, :, :HD],
            preferred_element_type=jnp.float32,
        )
        * score_scale
    )
    fresh_scores = (
        jnp.einsum(
            "smhd,snd->hsmn",
            slot_queries,
            slot_fresh[:, :, :HD],
            preferred_element_type=jnp.float32,
        )
        * score_scale
    )
    prefix_scores = jnp.where(prefix_mask[None], prefix_scores, -jnp.inf)
    fresh_scores = jnp.where(fresh_mask[None], fresh_scores, -jnp.inf)
    row_peak = jnp.maximum(jnp.max(prefix_scores, axis=3), jnp.max(fresh_scores, axis=3))
    prefix_weights = jnp.exp(prefix_scores - row_peak[..., None])
    fresh_weights = jnp.exp(fresh_scores - row_peak[..., None])
    denominator = jnp.sum(prefix_weights, axis=3) + jnp.sum(fresh_weights, axis=3)
    mixed_values = jnp.einsum(
        "hsmk,skd->smhd",
        prefix_weights.astype(jnp.bfloat16),
        prefix_blocks[:, :, HD:],
        preferred_element_type=jnp.float32,
    )
    mixed_values = mixed_values + jnp.einsum(
        "hsmn,snd->smhd",
        fresh_weights.astype(jnp.bfloat16),
        slot_fresh[:, :, HD:],
        preferred_element_type=jnp.float32,
    )
    slot_attended = (mixed_values / jnp.transpose(denominator, (1, 2, 0))[..., None]).astype(
        jnp.bfloat16
    )
    slot_attended = slot_attended.reshape(sessions * slot_rows, heads_local * HD)
    back_index = row_slot * slot_rows + row_ids - jnp.take(starts, row_slot, axis=0)
    attended = jnp.take(slot_attended, back_index, axis=0)
    gathered = lax.all_to_all(
        jnp.broadcast_to(attended[None], (replicas,) + attended.shape),
        "replica",
        split_axis=0,
        concat_axis=0,
        tiled=True,
    ).reshape(replicas * rows_here, attended.shape[1])
    partial_out = jnp.dot(
        gathered,
        out_weight,
        preferred_element_type=jnp.float32,
    )
    all_rows = partial_out.shape[0]
    width = partial_out.shape[1]
    part_rows = all_rows // tensors
    head_parts = lax.all_to_all(
        partial_out.astype(jnp.bfloat16).reshape(tensors, part_rows, width),
        "tensor",
        split_axis=0,
        concat_axis=0,
        tiled=True,
    )
    head_sum = jnp.sum(head_parts.astype(jnp.float32), axis=0)
    my_residual = lax.dynamic_slice_in_dim(residual, tensor_idx * part_rows, part_rows, 0)
    carried = my_residual.astype(jnp.float32) + head_sum
    gain_row = norm_gain.astype(jnp.float32)
    squares = jnp.sum(carried * carried, axis=1)
    step = 1
    while step < replicas:
        squares = squares + lax.ppermute(
            squares, "replica", [(i, i ^ step) for i in range(replicas)]
        )
        step *= 2
    normed_part = (
        carried * lax.rsqrt(squares / D + EPSILON)[:, None] * gain_row[None, :]
    ).astype(jnp.bfloat16)
    normed = lax.all_gather(normed_part, "tensor", axis=0, tiled=True)
    weights_local = gate_up.reshape(gate_up.shape[0], 2 * gate_up.shape[2])
    slab = jnp.dot(normed, weights_local, preferred_element_type=jnp.float32)
    slab_parts = lax.all_to_all(
        slab.astype(jnp.bfloat16).reshape(replicas, rows_here, slab.shape[1]),
        "replica",
        split_axis=0,
        concat_axis=0,
        tiled=True,
    )
    summed = jnp.sum(slab_parts.astype(jnp.float32), axis=0)
    ff_here = gate_up.shape[2]
    gate = summed[:, :ff_here]
    up = summed[:, ff_here:]
    return (jax.nn.silu(gate) * up).astype(jnp.bfloat16)


def solution(mesh):
    placed = (
        P("replica", "tensor"),
        P("replica", None),
        P(("replica", "tensor"), None, None),
        P(),
        P(),
        P(),
        P(),
        P("tensor", "replica"),
        P(None, "replica"),
        P("replica"),
        P("replica", None, "tensor"),
    )
    return jax.shard_map(
        per_device, mesh=mesh, in_specs=placed, out_specs=P("replica", "tensor"), check_vma=False
    )
```

```python
import jax
import jax.numpy as jnp
import numpy as np
from jax import lax
from jax.sharding import PartitionSpec as P

D = 16384
HD = 128
HEADS = 64
KVH = 4
PAGE = 64
SHARE = 1
ROWS = 128
GROUP = 16


EPSILON = 1e-05


def per_device(
    queries,
    new_kv,
    kv_pool,
    anchor,
    page_table,
    prefix_len,
    turn_rows,
    out_weight,
    residual,
    norm_gain,
    gate_up,
):
    replicas = lax.axis_size("replica")
    tensors = lax.axis_size("tensor")
    replica_idx = lax.axis_index("replica")
    tensor_idx = lax.axis_index("tensor")
    sessions = SHARE * replicas
    heads_local = HEADS // tensors
    pair_width = 2 * HD
    cached_len = tensors * PAGE
    owner_head = np.arange(tensors) * heads_local // GROUP
    from_here = lax.dynamic_slice_in_dim(anchor, replica_idx * SHARE, SHARE, 1)
    table_rows = lax.dynamic_slice_in_dim(page_table, replica_idx * sessions, sessions, 0)
    my_column = lax.dynamic_slice_in_dim(table_rows, tensor_idx, 1, 1)[:, 0]
    page_index = jnp.take(my_column, from_here.reshape(-1), axis=0)
    chosen = jnp.take(kv_pool, page_index, axis=0).reshape(replicas, SHARE, PAGE, KVH, pair_width)
    half = PAGE // 2
    lanes_per_head = tensors // KVH
    outgoing = jnp.transpose(
        chosen.reshape(replicas, 2, half, KVH, pair_width), (0, 3, 1, 2, 4)
    )
    outgoing = jnp.broadcast_to(
        outgoing[:, :, None],
        (replicas, KVH, lanes_per_head // 2, 2, half, pair_width),
    ).reshape(replicas * tensors, SHARE, half, pair_width)
    arrived = lax.all_to_all(
        outgoing, ("replica", "tensor"), split_axis=0, concat_axis=0, tiled=True
    )
    partner = lax.ppermute(arrived, "tensor", [(i, i ^ 1) for i in range(tensors)])
    mine_first = (tensor_idx % 2) == 0
    low_half = jnp.where(mine_first, arrived, partner)
    high_half = jnp.where(mine_first, partner, arrived)
    arrived = jnp.concatenate([low_half, high_half], axis=2)
    arrived = arrived.reshape(replicas, tensors, SHARE, PAGE, pair_width)
    prefix_blocks = jnp.transpose(arrived, (0, 2, 1, 3, 4)).reshape(
        sessions, cached_len, pair_width
    )
    kv_group = tensor_idx * heads_local // GROUP
    fresh_pair = lax.dynamic_slice_in_dim(new_kv, kv_group * pair_width, pair_width, 1)
    rows_here = queries.shape[0]
    slot_rows = ROWS // 4
    query_heads = queries.reshape(rows_here, heads_local, HD)
    counts = lax.dynamic_slice_in_dim(turn_rows, replica_idx, 1, 0)[0]
    bounds = jnp.cumsum(counts, dtype=jnp.int32)
    starts = bounds - counts
    row_ids = jnp.arange(rows_here, dtype=jnp.int32)
    row_slot = jnp.sum(
        (row_ids[:, None] >= bounds[None, :]).astype(jnp.int32), axis=1, dtype=jnp.int32
    )
    offsets = jnp.arange(slot_rows, dtype=jnp.int32)
    padded_index = jnp.minimum(starts[:, None] + offsets[None, :], rows_here - 1).reshape(-1)
    slot_queries = jnp.take(query_heads, padded_index, axis=0).reshape(
        sessions, slot_rows, heads_local, HD
    )
    slot_fresh = jnp.take(fresh_pair, padded_index, axis=0).reshape(sessions, slot_rows, pair_width)
    lengths = lax.dynamic_slice_in_dim(prefix_len, replica_idx * sessions, sessions, 0)
    key_pos = jnp.arange(cached_len, dtype=jnp.int32)
    prefix_mask = (key_pos[None, :] < lengths[:, None])[:, None, :]
    fresh_mask = (offsets[None, None, :] <= offsets[None, :, None]) & (
        offsets[None, None, :] < counts[:, None, None]
    )
    score_scale = HD ** (-0.5)
    prefix_scores = (
        jnp.einsum(
            "smhd,skd->hsmk",
            slot_queries,
            prefix_blocks[:, :, :HD],
            preferred_element_type=jnp.float32,
        )
        * score_scale
    )
    fresh_scores = (
        jnp.einsum(
            "smhd,snd->hsmn",
            slot_queries,
            slot_fresh[:, :, :HD],
            preferred_element_type=jnp.float32,
        )
        * score_scale
    )
    prefix_scores = jnp.where(prefix_mask[None], prefix_scores, -jnp.inf)
    fresh_scores = jnp.where(fresh_mask[None], fresh_scores, -jnp.inf)
    row_peak = jnp.maximum(jnp.max(prefix_scores, axis=3), jnp.max(fresh_scores, axis=3))
    prefix_weights = jnp.exp(prefix_scores - row_peak[..., None])
    fresh_weights = jnp.exp(fresh_scores - row_peak[..., None])
    denominator = jnp.sum(prefix_weights, axis=3) + jnp.sum(fresh_weights, axis=3)
    mixed_values = jnp.einsum(
        "hsmk,skd->smhd",
        prefix_weights.astype(jnp.bfloat16),
        prefix_blocks[:, :, HD:],
        preferred_element_type=jnp.float32,
    )
    mixed_values = mixed_values + jnp.einsum(
        "hsmn,snd->smhd",
        fresh_weights.astype(jnp.bfloat16),
        slot_fresh[:, :, HD:],
        preferred_element_type=jnp.float32,
    )
    slot_attended = (mixed_values / jnp.transpose(denominator, (1, 2, 0))[..., None]).astype(
        jnp.bfloat16
    )
    slot_attended = slot_attended.reshape(sessions * slot_rows, heads_local * HD)
    back_index = row_slot * slot_rows + row_ids - jnp.take(starts, row_slot, axis=0)
    attended = jnp.take(slot_attended, back_index, axis=0)
    gathered = lax.all_to_all(
        jnp.broadcast_to(attended[None], (replicas,) + attended.shape),
        "replica",
        split_axis=0,
        concat_axis=0,
        tiled=True,
    ).reshape(replicas * rows_here, attended.shape[1])
    partial_out = jnp.dot(
        gathered,
        out_weight,
        preferred_element_type=jnp.float32,
    )
    all_rows = partial_out.shape[0]
    width = partial_out.shape[1]
    part_rows = all_rows // tensors
    head_parts = lax.all_to_all(
        partial_out.astype(jnp.bfloat16).reshape(tensors, part_rows, width),
        "tensor",
        split_axis=0,
        concat_axis=0,
        tiled=True,
    )
    head_sum = jnp.sum(head_parts.astype(jnp.float32), axis=0)
    my_residual = lax.dynamic_slice_in_dim(residual, tensor_idx * part_rows, part_rows, 0)
    carried = my_residual.astype(jnp.float32) + head_sum
    gain_row = norm_gain.astype(jnp.float32)
    own_squares = jnp.sum(carried * carried, axis=1)
    received = [own_squares] + [
        lax.ppermute(own_squares, "replica", [(i, i ^ k) for i in range(replicas)])
        for k in range(1, replicas)
    ]
    by_source = jnp.take(
        jnp.stack(received), jnp.arange(replicas, dtype=jnp.int32) ^ replica_idx, axis=0
    )
    squares = jnp.sum(by_source, axis=0)
    normed_part = (
        carried * lax.rsqrt(squares / D + EPSILON)[:, None] * gain_row[None, :]
    ).astype(jnp.bfloat16)
    normed = lax.all_gather(normed_part, "tensor", axis=0, tiled=True)
    weights_local = gate_up.reshape(gate_up.shape[0], 2 * gate_up.shape[2])
    slab = jnp.dot(normed, weights_local, preferred_element_type=jnp.float32)
    slab_parts = lax.all_to_all(
        slab.astype(jnp.bfloat16).reshape(replicas, rows_here, slab.shape[1]),
        "replica",
        split_axis=0,
        concat_axis=0,
        tiled=True,
    )
    summed = jnp.sum(slab_parts.astype(jnp.float32), axis=0)
    ff_here = gate_up.shape[2]
    gate = summed[:, :ff_here]
    up = summed[:, ff_here:]
    return (jax.nn.silu(gate) * up).astype(jnp.bfloat16)


def solution(mesh):
    placed = (
        P("replica", "tensor"),
        P("replica", None),
        P(("replica", "tensor"), None, None),
        P(),
        P(),
        P(),
        P(),
        P("tensor", "replica"),
        P(None, "replica"),
        P("replica"),
        P("replica", None, "tensor"),
    )
    return jax.shard_map(
        per_device, mesh=mesh, in_specs=placed, out_specs=P("replica", "tensor"), check_vma=False
    )
```

```python
import jax
import jax.numpy as jnp
import numpy as np
from jax import lax
from jax.sharding import PartitionSpec as P

D = 16384
HD = 128
HEADS = 64
KVH = 4
PAGE = 64
SHARE = 1
ROWS = 128
GROUP = 16


EPSILON = 1e-05


def per_device(
    queries,
    new_kv,
    kv_pool,
    anchor,
    page_table,
    prefix_len,
    turn_rows,
    out_weight,
    residual,
    norm_gain,
    gate_up,
):
    replicas = lax.axis_size("replica")
    tensors = lax.axis_size("tensor")
    replica_idx = lax.axis_index("replica")
    tensor_idx = lax.axis_index("tensor")
    sessions = SHARE * replicas
    heads_local = HEADS // tensors
    pair_width = 2 * HD
    cached_len = tensors * PAGE
    owner_head = np.arange(tensors) * heads_local // GROUP
    from_here = lax.dynamic_slice_in_dim(anchor, replica_idx * SHARE, SHARE, 1)
    table_rows = lax.dynamic_slice_in_dim(page_table, replica_idx * sessions, sessions, 0)
    my_column = lax.dynamic_slice_in_dim(table_rows, tensor_idx, 1, 1)[:, 0]
    page_index = jnp.take(my_column, from_here.reshape(-1), axis=0)
    chosen = jnp.take(kv_pool, page_index, axis=0).reshape(replicas, SHARE, PAGE, KVH, pair_width)
    half = PAGE // 2
    lanes_per_head = tensors // KVH
    outgoing = jnp.transpose(
        chosen.reshape(replicas, 2, half, KVH, pair_width), (0, 3, 1, 2, 4)
    )
    outgoing = jnp.broadcast_to(
        outgoing[:, :, None],
        (replicas, KVH, lanes_per_head // 2, 2, half, pair_width),
    ).reshape(replicas * tensors, SHARE, half, pair_width)
    arrived = lax.all_to_all(
        outgoing, ("replica", "tensor"), split_axis=0, concat_axis=0, tiled=True
    )
    partner = lax.ppermute(arrived, "tensor", [(i, i ^ 1) for i in range(tensors)])
    arrived = jnp.concatenate([arrived, partner], axis=2)
    arrived = arrived.reshape(replicas, tensors, SHARE, PAGE, pair_width)
    prefix_blocks = jnp.transpose(arrived, (0, 2, 1, 3, 4)).reshape(
        sessions, cached_len, pair_width
    )
    kv_group = tensor_idx * heads_local // GROUP
    fresh_pair = lax.dynamic_slice_in_dim(new_kv, kv_group * pair_width, pair_width, 1)
    rows_here = queries.shape[0]
    slot_rows = ROWS // 4
    query_heads = queries.reshape(rows_here, heads_local, HD)
    counts = lax.dynamic_slice_in_dim(turn_rows, replica_idx, 1, 0)[0]
    bounds = jnp.cumsum(counts, dtype=jnp.int32)
    starts = bounds - counts
    row_ids = jnp.arange(rows_here, dtype=jnp.int32)
    row_slot = jnp.sum(
        (row_ids[:, None] >= bounds[None, :]).astype(jnp.int32), axis=1, dtype=jnp.int32
    )
    offsets = jnp.arange(slot_rows, dtype=jnp.int32)
    padded_index = jnp.minimum(starts[:, None] + offsets[None, :], rows_here - 1).reshape(-1)
    slot_queries = jnp.take(query_heads, padded_index, axis=0).reshape(
        sessions, slot_rows, heads_local, HD
    )
    slot_fresh = jnp.take(fresh_pair, padded_index, axis=0).reshape(sessions, slot_rows, pair_width)
    lengths = lax.dynamic_slice_in_dim(prefix_len, replica_idx * sessions, sessions, 0)
    key_ids = jnp.arange(cached_len, dtype=jnp.int32)
    key_pos = (key_ids // PAGE) * PAGE + (key_ids % PAGE + (tensor_idx % 2) * half) % PAGE
    prefix_mask = (key_pos[None, :] < lengths[:, None])[:, None, :]
    fresh_mask = (offsets[None, None, :] <= offsets[None, :, None]) & (
        offsets[None, None, :] < counts[:, None, None]
    )
    score_scale = HD ** (-0.5)
    prefix_scores = (
        jnp.einsum(
            "smhd,skd->hsmk",
            slot_queries,
            prefix_blocks[:, :, :HD],
            preferred_element_type=jnp.float32,
        )
        * score_scale
    )
    fresh_scores = (
        jnp.einsum(
            "smhd,snd->hsmn",
            slot_queries,
            slot_fresh[:, :, :HD],
            preferred_element_type=jnp.float32,
        )
        * score_scale
    )
    prefix_scores = jnp.where(prefix_mask[None], prefix_scores, -jnp.inf)
    fresh_scores = jnp.where(fresh_mask[None], fresh_scores, -jnp.inf)
    row_peak = jnp.maximum(jnp.max(prefix_scores, axis=3), jnp.max(fresh_scores, axis=3))
    prefix_weights = jnp.exp(prefix_scores - row_peak[..., None])
    fresh_weights = jnp.exp(fresh_scores - row_peak[..., None])
    denominator = jnp.sum(prefix_weights, axis=3) + jnp.sum(fresh_weights, axis=3)
    mixed_values = jnp.einsum(
        "hsmk,skd->smhd",
        prefix_weights.astype(jnp.bfloat16),
        prefix_blocks[:, :, HD:],
        preferred_element_type=jnp.float32,
    )
    mixed_values = mixed_values + jnp.einsum(
        "hsmn,snd->smhd",
        fresh_weights.astype(jnp.bfloat16),
        slot_fresh[:, :, HD:],
        preferred_element_type=jnp.float32,
    )
    slot_attended = (mixed_values / jnp.transpose(denominator, (1, 2, 0))[..., None]).astype(
        jnp.bfloat16
    )
    slot_attended = slot_attended.reshape(sessions * slot_rows, heads_local * HD)
    back_index = row_slot * slot_rows + row_ids - jnp.take(starts, row_slot, axis=0)
    attended = jnp.take(slot_attended, back_index, axis=0)
    gathered = lax.all_to_all(
        jnp.broadcast_to(attended[None], (replicas,) + attended.shape),
        "replica",
        split_axis=0,
        concat_axis=0,
        tiled=True,
    ).reshape(replicas * rows_here, attended.shape[1])
    partial_out = jnp.dot(
        gathered,
        out_weight,
        preferred_element_type=jnp.float32,
    )
    all_rows = partial_out.shape[0]
    width = partial_out.shape[1]
    part_rows = all_rows // tensors
    head_parts = lax.all_to_all(
        partial_out.astype(jnp.bfloat16).reshape(tensors, part_rows, width),
        "tensor",
        split_axis=0,
        concat_axis=0,
        tiled=True,
    )
    head_sum = jnp.sum(head_parts.astype(jnp.float32), axis=0)
    my_residual = lax.dynamic_slice_in_dim(residual, tensor_idx * part_rows, part_rows, 0)
    carried = my_residual.astype(jnp.float32) + head_sum
    gain_row = norm_gain.astype(jnp.float32)
    squares = jnp.sum(carried * carried, axis=1)
    step = 1
    while step < replicas:
        squares = squares + lax.ppermute(
            squares, "replica", [(i, i ^ step) for i in range(replicas)]
        )
        step *= 2
    normed_part = (
        carried * lax.rsqrt(squares / D + EPSILON)[:, None] * gain_row[None, :]
    ).astype(jnp.bfloat16)
    normed = lax.all_gather(normed_part, "tensor", axis=0, tiled=True)
    weights_local = gate_up.reshape(gate_up.shape[0], 2 * gate_up.shape[2])
    slab = jnp.dot(normed, weights_local, preferred_element_type=jnp.float32)
    slab_parts = lax.all_to_all(
        slab.astype(jnp.bfloat16).reshape(replicas, rows_here, slab.shape[1]),
        "replica",
        split_axis=0,
        concat_axis=0,
        tiled=True,
    )
    summed = jnp.sum(slab_parts.astype(jnp.float32), axis=0)
    ff_here = gate_up.shape[2]
    gate = summed[:, :ff_here]
    up = summed[:, ff_here:]
    return (jax.nn.silu(gate) * up).astype(jnp.bfloat16)


def solution(mesh):
    placed = (
        P("replica", "tensor"),
        P("replica", None),
        P(("replica", "tensor"), None, None),
        P(),
        P(),
        P(),
        P(),
        P("tensor", "replica"),
        P(None, "replica"),
        P("replica"),
        P("replica", None, "tensor"),
    )
    return jax.shard_map(
        per_device, mesh=mesh, in_specs=placed, out_specs=P("replica", "tensor"), check_vma=False
    )
```

```python
import jax
import jax.numpy as jnp
import numpy as np
from jax import lax
from jax.sharding import PartitionSpec as P

D = 16384
HD = 128
HEADS = 64
KVH = 4
PAGE = 64
SHARE = 1
ROWS = 128
GROUP = 16


EPSILON = 1e-05


def per_device(
    queries,
    new_kv,
    kv_pool,
    anchor,
    page_table,
    prefix_len,
    turn_rows,
    out_weight,
    residual,
    norm_gain,
    gate_up,
):
    replicas = lax.axis_size("replica")
    tensors = lax.axis_size("tensor")
    replica_idx = lax.axis_index("replica")
    tensor_idx = lax.axis_index("tensor")
    sessions = SHARE * replicas
    heads_local = HEADS // tensors
    pair_width = 2 * HD
    cached_len = tensors * PAGE
    owner_head = np.arange(tensors) * heads_local // GROUP
    from_here = lax.dynamic_slice_in_dim(anchor, replica_idx * SHARE, SHARE, 1)
    table_rows = lax.dynamic_slice_in_dim(page_table, replica_idx * sessions, sessions, 0)
    my_column = lax.dynamic_slice_in_dim(table_rows, tensor_idx, 1, 1)[:, 0]
    page_index = jnp.take(my_column, from_here.reshape(-1), axis=0)
    chosen = jnp.take(kv_pool, page_index, axis=0).reshape(replicas, SHARE, PAGE, KVH, pair_width)
    half = PAGE // 2
    lanes_per_head = tensors // KVH
    outgoing = jnp.transpose(
        chosen.reshape(replicas, 2, half, KVH, pair_width), (0, 3, 1, 2, 4)
    )
    outgoing = jnp.broadcast_to(
        outgoing[:, :, None],
        (replicas, KVH, lanes_per_head // 2, 2, half, pair_width),
    ).reshape(replicas * tensors, SHARE, half, pair_width)
    arrived = lax.all_to_all(
        outgoing, ("replica", "tensor"), split_axis=0, concat_axis=0, tiled=True
    )
    weights_local = gate_up.reshape(gate_up.shape[0], 2 * gate_up.shape[2])
    arrived, weights_local = lax.optimization_barrier((arrived, weights_local))
    partner = lax.ppermute(arrived, "tensor", [(i, i ^ 1) for i in range(tensors)])
    mine_first = (tensor_idx % 2) == 0
    low_half = jnp.where(mine_first, arrived, partner)
    high_half = jnp.where(mine_first, partner, arrived)
    arrived = jnp.concatenate([low_half, high_half], axis=2)
    arrived = arrived.reshape(replicas, tensors, SHARE, PAGE, pair_width)
    prefix_blocks = jnp.transpose(arrived, (0, 2, 1, 3, 4)).reshape(
        sessions, cached_len, pair_width
    )
    kv_group = tensor_idx * heads_local // GROUP
    fresh_pair = lax.dynamic_slice_in_dim(new_kv, kv_group * pair_width, pair_width, 1)
    rows_here = queries.shape[0]
    slot_rows = ROWS // 4
    query_heads = queries.reshape(rows_here, heads_local, HD)
    counts = lax.dynamic_slice_in_dim(turn_rows, replica_idx, 1, 0)[0]
    bounds = jnp.cumsum(counts, dtype=jnp.int32)
    starts = bounds - counts
    row_ids = jnp.arange(rows_here, dtype=jnp.int32)
    row_slot = jnp.sum(
        (row_ids[:, None] >= bounds[None, :]).astype(jnp.int32), axis=1, dtype=jnp.int32
    )
    offsets = jnp.arange(slot_rows, dtype=jnp.int32)
    padded_index = jnp.minimum(starts[:, None] + offsets[None, :], rows_here - 1).reshape(-1)
    slot_queries = jnp.take(query_heads, padded_index, axis=0).reshape(
        sessions, slot_rows, heads_local, HD
    )
    slot_fresh = jnp.take(fresh_pair, padded_index, axis=0).reshape(sessions, slot_rows, pair_width)
    lengths = lax.dynamic_slice_in_dim(prefix_len, replica_idx * sessions, sessions, 0)
    key_pos = jnp.arange(cached_len, dtype=jnp.int32)
    prefix_mask = (key_pos[None, :] < lengths[:, None])[:, None, :]
    fresh_mask = (offsets[None, None, :] <= offsets[None, :, None]) & (
        offsets[None, None, :] < counts[:, None, None]
    )
    score_scale = HD ** (-0.5)
    prefix_scores = (
        jnp.einsum(
            "smhd,skd->hsmk",
            slot_queries,
            prefix_blocks[:, :, :HD],
            preferred_element_type=jnp.float32,
        )
        * score_scale
    )
    fresh_scores = (
        jnp.einsum(
            "smhd,snd->hsmn",
            slot_queries,
            slot_fresh[:, :, :HD],
            preferred_element_type=jnp.float32,
        )
        * score_scale
    )
    prefix_scores = jnp.where(prefix_mask[None], prefix_scores, -jnp.inf)
    fresh_scores = jnp.where(fresh_mask[None], fresh_scores, -jnp.inf)
    row_peak = jnp.maximum(jnp.max(prefix_scores, axis=3), jnp.max(fresh_scores, axis=3))
    prefix_weights = jnp.exp(prefix_scores - row_peak[..., None])
    fresh_weights = jnp.exp(fresh_scores - row_peak[..., None])
    denominator = jnp.sum(prefix_weights, axis=3) + jnp.sum(fresh_weights, axis=3)
    mixed_values = jnp.einsum(
        "hsmk,skd->smhd",
        prefix_weights.astype(jnp.bfloat16),
        prefix_blocks[:, :, HD:],
        preferred_element_type=jnp.float32,
    )
    mixed_values = mixed_values + jnp.einsum(
        "hsmn,snd->smhd",
        fresh_weights.astype(jnp.bfloat16),
        slot_fresh[:, :, HD:],
        preferred_element_type=jnp.float32,
    )
    slot_attended = (mixed_values / jnp.transpose(denominator, (1, 2, 0))[..., None]).astype(
        jnp.bfloat16
    )
    slot_attended = slot_attended.reshape(sessions * slot_rows, heads_local * HD)
    back_index = row_slot * slot_rows + row_ids - jnp.take(starts, row_slot, axis=0)
    attended = jnp.take(slot_attended, back_index, axis=0)
    gathered = lax.all_to_all(
        jnp.broadcast_to(attended[None], (replicas,) + attended.shape),
        "replica",
        split_axis=0,
        concat_axis=0,
        tiled=True,
    ).reshape(replicas * rows_here, attended.shape[1])
    partial_out = jnp.dot(
        gathered,
        out_weight,
        preferred_element_type=jnp.float32,
    )
    all_rows = partial_out.shape[0]
    width = partial_out.shape[1]
    part_rows = all_rows // tensors
    head_parts = lax.all_to_all(
        partial_out.astype(jnp.bfloat16).reshape(tensors, part_rows, width),
        "tensor",
        split_axis=0,
        concat_axis=0,
        tiled=True,
    )
    head_sum = jnp.sum(head_parts.astype(jnp.float32), axis=0)
    my_residual = lax.dynamic_slice_in_dim(residual, tensor_idx * part_rows, part_rows, 0)
    carried = my_residual.astype(jnp.float32) + head_sum
    gain_row = norm_gain.astype(jnp.float32)
    squares = jnp.sum(carried * carried, axis=1)
    step = 1
    while step < replicas:
        squares = squares + lax.ppermute(
            squares, "replica", [(i, i ^ step) for i in range(replicas)]
        )
        step *= 2
    normed_part = (
        carried * lax.rsqrt(squares / D + EPSILON)[:, None] * gain_row[None, :]
    ).astype(jnp.bfloat16)
    normed = lax.all_gather(normed_part, "tensor", axis=0, tiled=True)
    slab = jnp.dot(normed, weights_local, preferred_element_type=jnp.float32)
    slab_parts = lax.all_to_all(
        slab.astype(jnp.bfloat16).reshape(replicas, rows_here, slab.shape[1]),
        "replica",
        split_axis=0,
        concat_axis=0,
        tiled=True,
    )
    summed = jnp.sum(slab_parts.astype(jnp.float32), axis=0)
    ff_here = gate_up.shape[2]
    gate = summed[:, :ff_here]
    up = summed[:, ff_here:]
    return (jax.nn.silu(gate) * up).astype(jnp.bfloat16)


def solution(mesh):
    placed = (
        P("replica", "tensor"),
        P("replica", None),
        P(("replica", "tensor"), None, None),
        P(),
        P(),
        P(),
        P(),
        P("tensor", "replica"),
        P(None, "replica"),
        P("replica"),
        P("replica", None, "tensor"),
    )
    return jax.shard_map(
        per_device, mesh=mesh, in_specs=placed, out_specs=P("replica", "tensor"), check_vma=False
    )
```

```python
import jax
import jax.numpy as jnp
import numpy as np
from jax import lax
from jax.sharding import PartitionSpec as P

D = 16384
HD = 128
HEADS = 64
KVH = 4
PAGE = 64
SHARE = 1
ROWS = 128
GROUP = 16


EPSILON = 1e-05


def per_device(
    queries,
    new_kv,
    kv_pool,
    anchor,
    page_table,
    prefix_len,
    turn_rows,
    out_weight,
    residual,
    norm_gain,
    gate_up,
):
    replicas = lax.axis_size("replica")
    tensors = lax.axis_size("tensor")
    replica_idx = lax.axis_index("replica")
    tensor_idx = lax.axis_index("tensor")
    sessions = SHARE * replicas
    heads_local = HEADS // tensors
    pair_width = 2 * HD
    cached_len = tensors * PAGE
    owner_head = np.arange(tensors) * heads_local // GROUP
    from_here = lax.dynamic_slice_in_dim(anchor, replica_idx * SHARE, SHARE, 1)
    table_rows = lax.dynamic_slice_in_dim(page_table, replica_idx * sessions, sessions, 0)
    my_column = lax.dynamic_slice_in_dim(table_rows, tensor_idx, 1, 1)[:, 0]
    page_index = jnp.take(my_column, from_here.reshape(-1), axis=0)
    chosen = jnp.take(kv_pool, page_index, axis=0).reshape(replicas, SHARE, PAGE, KVH, pair_width)
    half = PAGE // 2
    lanes_per_head = tensors // KVH
    outgoing = jnp.transpose(
        chosen.reshape(replicas, 2, half, KVH, pair_width), (0, 3, 1, 2, 4)
    )
    outgoing = jnp.broadcast_to(
        outgoing[:, :, None],
        (replicas, KVH, lanes_per_head // 2, 2, half, pair_width),
    ).reshape(replicas * tensors, SHARE, half, pair_width)
    arrived = lax.all_to_all(
        outgoing, ("replica", "tensor"), split_axis=0, concat_axis=0, tiled=True
    )
    partner = lax.ppermute(arrived, "tensor", [(i, i ^ 1) for i in range(tensors)])
    mine_first = (tensor_idx % 2) == 0
    low_half = jnp.where(mine_first, arrived, partner)
    high_half = jnp.where(mine_first, partner, arrived)
    arrived = jnp.concatenate([low_half, high_half], axis=2)
    arrived = arrived.reshape(replicas, tensors, SHARE, PAGE, pair_width)
    prefix_blocks = jnp.transpose(arrived, (0, 2, 1, 3, 4)).reshape(
        sessions, cached_len, pair_width
    )
    kv_group = tensor_idx * heads_local // GROUP
    fresh_pair = lax.dynamic_slice_in_dim(new_kv, kv_group * pair_width, pair_width, 1)
    rows_here = queries.shape[0]
    slot_rows = ROWS // 4
    query_heads = queries.reshape(rows_here, heads_local, HD)
    counts = lax.dynamic_slice_in_dim(turn_rows, replica_idx, 1, 0)[0]
    bounds = jnp.cumsum(counts, dtype=jnp.int32)
    starts = bounds - counts
    row_ids = jnp.arange(rows_here, dtype=jnp.int32)
    row_slot = jnp.sum(
        (row_ids[:, None] >= bounds[None, :]).astype(jnp.int32), axis=1, dtype=jnp.int32
    )
    offsets = jnp.arange(slot_rows, dtype=jnp.int32)
    padded_index = jnp.minimum(starts[:, None] + offsets[None, :], rows_here - 1).reshape(-1)
    slot_queries = jnp.take(query_heads, padded_index, axis=0).reshape(
        sessions, slot_rows, heads_local, HD
    )
    slot_fresh = jnp.take(fresh_pair, padded_index, axis=0).reshape(sessions, slot_rows, pair_width)
    lengths = lax.dynamic_slice_in_dim(prefix_len, replica_idx * sessions, sessions, 0)
    key_pos = jnp.arange(cached_len, dtype=jnp.int32)
    prefix_mask = (key_pos[None, :] < lengths[:, None])[:, None, :]
    fresh_mask = (offsets[None, None, :] <= offsets[None, :, None]) & (
        offsets[None, None, :] < counts[:, None, None]
    )
    score_scale = HD ** (-0.5)
    prefix_scores = (
        jnp.einsum(
            "smhd,skd->hsmk",
            slot_queries,
            prefix_blocks[:, :, :HD],
            preferred_element_type=jnp.float32,
        )
        * score_scale
    )
    fresh_scores = (
        jnp.einsum(
            "smhd,snd->hsmn",
            slot_queries,
            slot_fresh[:, :, :HD],
            preferred_element_type=jnp.float32,
        )
        * score_scale
    )
    prefix_scores = jnp.where(prefix_mask[None], prefix_scores, -jnp.inf)
    fresh_scores = jnp.where(fresh_mask[None], fresh_scores, -jnp.inf)
    row_peak = jnp.maximum(jnp.max(prefix_scores, axis=3), jnp.max(fresh_scores, axis=3))
    prefix_weights = jnp.exp(prefix_scores - row_peak[..., None])
    fresh_weights = jnp.exp(fresh_scores - row_peak[..., None])
    denominator = jnp.sum(prefix_weights, axis=3) + jnp.sum(fresh_weights, axis=3)
    mixed_values = jnp.einsum(
        "hsmk,skd->smhd",
        prefix_weights.astype(jnp.bfloat16),
        prefix_blocks[:, :, HD:],
        preferred_element_type=jnp.float32,
    )
    mixed_values = mixed_values + jnp.einsum(
        "hsmn,snd->smhd",
        fresh_weights.astype(jnp.bfloat16),
        slot_fresh[:, :, HD:],
        preferred_element_type=jnp.float32,
    )
    slot_attended = (mixed_values / jnp.transpose(denominator, (1, 2, 0))[..., None]).astype(
        jnp.bfloat16
    )
    slot_attended = slot_attended.reshape(sessions * slot_rows, heads_local * HD)
    back_index = row_slot * slot_rows + row_ids - jnp.take(starts, row_slot, axis=0)
    attended = jnp.take(slot_attended, back_index, axis=0)
    gathered = lax.all_to_all(
        jnp.broadcast_to(attended[None], (replicas,) + attended.shape),
        "replica",
        split_axis=0,
        concat_axis=0,
        tiled=True,
    ).reshape(replicas * rows_here, attended.shape[1])
    partial_out = jnp.dot(
        gathered,
        out_weight,
        preferred_element_type=jnp.float32,
    )
    all_rows = partial_out.shape[0]
    width = partial_out.shape[1]
    part_rows = all_rows // tensors
    head_parts = lax.all_to_all(
        partial_out.astype(jnp.bfloat16).reshape(tensors, part_rows, width),
        "tensor",
        split_axis=0,
        concat_axis=0,
        tiled=True,
    )
    head_sum = jnp.sum(head_parts.astype(jnp.float32), axis=0)
    my_residual = lax.dynamic_slice_in_dim(residual, tensor_idx * part_rows, part_rows, 0)
    carried = my_residual.astype(jnp.float32) + head_sum
    gain_row = norm_gain.astype(jnp.float32)
    own_squares = jnp.sum(carried * carried, axis=1)
    squares = jnp.sum(
        lax.all_to_all(
            jnp.broadcast_to(own_squares[None], (replicas,) + own_squares.shape),
            "replica",
            split_axis=0,
            concat_axis=0,
            tiled=True,
        ),
        axis=0,
    )
    normed_part = (
        carried * lax.rsqrt(squares / D + EPSILON)[:, None] * gain_row[None, :]
    ).astype(jnp.bfloat16)
    normed = lax.all_gather(normed_part, "tensor", axis=0, tiled=True)
    weights_local = gate_up.reshape(gate_up.shape[0], 2 * gate_up.shape[2])
    slab = jnp.dot(normed, weights_local, preferred_element_type=jnp.float32)
    slab_parts = lax.all_to_all(
        slab.astype(jnp.bfloat16).reshape(replicas, rows_here, slab.shape[1]),
        "replica",
        split_axis=0,
        concat_axis=0,
        tiled=True,
    )
    summed = jnp.sum(slab_parts.astype(jnp.float32), axis=0)
    ff_here = gate_up.shape[2]
    gate = summed[:, :ff_here]
    up = summed[:, ff_here:]
    return (jax.nn.silu(gate) * up).astype(jnp.bfloat16)


def solution(mesh):
    placed = (
        P("replica", "tensor"),
        P("replica", None),
        P(("replica", "tensor"), None, None),
        P(),
        P(),
        P(),
        P(),
        P("tensor", "replica"),
        P(None, "replica"),
        P("replica"),
        P("replica", None, "tensor"),
    )
    return jax.shard_map(
        per_device, mesh=mesh, in_specs=placed, out_specs=P("replica", "tensor"), check_vma=False
    )
```

```python
import jax
import jax.numpy as jnp
import numpy as np
from jax import lax
from jax.sharding import PartitionSpec as P

D = 16384
HD = 128
HEADS = 64
KVH = 4
PAGE = 64
SHARE = 1
ROWS = 128
GROUP = 16


EPSILON = 1e-05


def per_device(
    queries,
    new_kv,
    kv_pool,
    anchor,
    page_table,
    prefix_len,
    turn_rows,
    out_weight,
    residual,
    norm_gain,
    gate_up,
):
    replicas = lax.axis_size(("zh", "y"))
    tensors = lax.axis_size(("x", "zl", "core"))
    replica_idx = lax.axis_index(("zh", "y"))
    tensor_idx = lax.axis_index(("x", "zl", "core"))
    sessions = SHARE * replicas
    heads_local = HEADS // tensors
    pair_width = 2 * HD
    cached_len = tensors * PAGE
    owner_head = np.arange(tensors) * heads_local // GROUP
    from_here = lax.dynamic_slice_in_dim(anchor, replica_idx * SHARE, SHARE, 1)
    table_rows = lax.dynamic_slice_in_dim(page_table, replica_idx * sessions, sessions, 0)
    my_column = lax.dynamic_slice_in_dim(table_rows, tensor_idx, 1, 1)[:, 0]
    page_index = jnp.take(my_column, from_here.reshape(-1), axis=0)
    chosen = jnp.take(kv_pool, page_index, axis=0).reshape(replicas, SHARE, PAGE, KVH, pair_width)
    half = PAGE // 2
    lanes_per_head = tensors // KVH
    outgoing = jnp.transpose(
        chosen.reshape(replicas, 2, half, KVH, pair_width), (0, 3, 1, 2, 4)
    )
    outgoing = jnp.broadcast_to(
        outgoing[:, :, None],
        (replicas, KVH, lanes_per_head // 2, 2, half, pair_width),
    ).reshape(replicas * tensors, SHARE, half, pair_width)
    arrived = lax.all_to_all(
        outgoing, ("zh", "y", "x", "zl", "core"), split_axis=0, concat_axis=0, tiled=True
    )
    partner = lax.ppermute(arrived, ("x", "zl", "core"), [(i, i ^ 1) for i in range(tensors)])
    mine_first = (tensor_idx % 2) == 0
    low_half = jnp.where(mine_first, arrived, partner)
    high_half = jnp.where(mine_first, partner, arrived)
    arrived = jnp.concatenate([low_half, high_half], axis=2)
    arrived = arrived.reshape(replicas, tensors, SHARE, PAGE, pair_width)
    prefix_blocks = jnp.transpose(arrived, (0, 2, 1, 3, 4)).reshape(
        sessions, cached_len, pair_width
    )
    kv_group = tensor_idx * heads_local // GROUP
    fresh_pair = lax.dynamic_slice_in_dim(new_kv, kv_group * pair_width, pair_width, 1)
    rows_here = queries.shape[0]
    slot_rows = ROWS // 4
    query_heads = queries.reshape(rows_here, heads_local, HD)
    counts = lax.dynamic_slice_in_dim(turn_rows, replica_idx, 1, 0)[0]
    bounds = jnp.cumsum(counts, dtype=jnp.int32)
    starts = bounds - counts
    row_ids = jnp.arange(rows_here, dtype=jnp.int32)
    row_slot = jnp.sum(
        (row_ids[:, None] >= bounds[None, :]).astype(jnp.int32), axis=1, dtype=jnp.int32
    )
    offsets = jnp.arange(slot_rows, dtype=jnp.int32)
    padded_index = jnp.minimum(starts[:, None] + offsets[None, :], rows_here - 1).reshape(-1)
    slot_queries = jnp.take(query_heads, padded_index, axis=0).reshape(
        sessions, slot_rows, heads_local, HD
    )
    slot_fresh = jnp.take(fresh_pair, padded_index, axis=0).reshape(sessions, slot_rows, pair_width)
    lengths = lax.dynamic_slice_in_dim(prefix_len, replica_idx * sessions, sessions, 0)
    key_pos = jnp.arange(cached_len, dtype=jnp.int32)
    prefix_mask = (key_pos[None, :] < lengths[:, None])[:, None, :]
    fresh_mask = (offsets[None, None, :] <= offsets[None, :, None]) & (
        offsets[None, None, :] < counts[:, None, None]
    )
    score_scale = HD ** (-0.5)
    prefix_scores = (
        jnp.einsum(
            "smhd,skd->hsmk",
            slot_queries,
            prefix_blocks[:, :, :HD],
            preferred_element_type=jnp.float32,
        )
        * score_scale
    )
    fresh_scores = (
        jnp.einsum(
            "smhd,snd->hsmn",
            slot_queries,
            slot_fresh[:, :, :HD],
            preferred_element_type=jnp.float32,
        )
        * score_scale
    )
    prefix_scores = jnp.where(prefix_mask[None], prefix_scores, -jnp.inf)
    fresh_scores = jnp.where(fresh_mask[None], fresh_scores, -jnp.inf)
    row_peak = jnp.maximum(jnp.max(prefix_scores, axis=3), jnp.max(fresh_scores, axis=3))
    prefix_weights = jnp.exp(prefix_scores - row_peak[..., None])
    fresh_weights = jnp.exp(fresh_scores - row_peak[..., None])
    denominator = jnp.sum(prefix_weights, axis=3) + jnp.sum(fresh_weights, axis=3)
    mixed_values = jnp.einsum(
        "hsmk,skd->smhd",
        prefix_weights.astype(jnp.bfloat16),
        prefix_blocks[:, :, HD:],
        preferred_element_type=jnp.float32,
    )
    mixed_values = mixed_values + jnp.einsum(
        "hsmn,snd->smhd",
        fresh_weights.astype(jnp.bfloat16),
        slot_fresh[:, :, HD:],
        preferred_element_type=jnp.float32,
    )
    slot_attended = (mixed_values / jnp.transpose(denominator, (1, 2, 0))[..., None]).astype(
        jnp.bfloat16
    )
    slot_attended = slot_attended.reshape(sessions * slot_rows, heads_local * HD)
    back_index = row_slot * slot_rows + row_ids - jnp.take(starts, row_slot, axis=0)
    attended = jnp.take(slot_attended, back_index, axis=0)
    gathered = lax.all_to_all(
        jnp.broadcast_to(attended[None], (replicas,) + attended.shape),
        ("zh", "y"),
        split_axis=0,
        concat_axis=0,
        tiled=True,
    ).reshape(replicas * rows_here, attended.shape[1])
    blocks = lax.axis_size(("x", "zl", "core"))
    pairs = blocks // 2
    block_of = (np.arange(blocks) % 2) * pairs + np.arange(blocks) // 2
    gathered = gathered.reshape(blocks, -1, gathered.shape[1])[block_of].reshape(
        gathered.shape
    )
    partial_out = jnp.dot(
        gathered,
        out_weight,
        preferred_element_type=jnp.float32,
    )
    all_rows = partial_out.shape[0]
    width = partial_out.shape[1]
    part_rows = all_rows // tensors
    head_parts = lax.all_to_all(
        partial_out.astype(jnp.bfloat16).reshape(tensors, part_rows, width),
        ("x", "zl", "core"),
        split_axis=0,
        concat_axis=0,
        tiled=True,
    )
    head_sum = jnp.sum(head_parts.astype(jnp.float32), axis=0)
    my_block = (tensor_idx % 2) * pairs + tensor_idx // 2
    my_residual = lax.dynamic_slice_in_dim(residual, my_block * part_rows, part_rows, 0)
    carried = my_residual.astype(jnp.float32) + head_sum
    gain_row = norm_gain.astype(jnp.float32)
    own_squares = jnp.sum(carried * carried, axis=1)
    squares = jnp.sum(
        lax.all_to_all(
            jnp.broadcast_to(own_squares[None], (replicas,) + own_squares.shape),
            ("zh", "y"),
            split_axis=0,
            concat_axis=0,
            tiled=True,
        ),
        axis=0,
    )
    normed_part = (
        carried * lax.rsqrt(squares / D + EPSILON)[:, None] * gain_row[None, :]
    ).astype(jnp.bfloat16)
    normed = lax.all_gather(
        lax.all_gather(normed_part, ("x", "zl"), axis=0, tiled=True), "core", axis=0, tiled=True
    )
    weights_local = gate_up.reshape(gate_up.shape[0], 2 * gate_up.shape[2])
    slab = jnp.dot(normed, weights_local, preferred_element_type=jnp.float32)
    slab_parts = lax.all_to_all(
        slab.astype(jnp.bfloat16).reshape(replicas, rows_here, slab.shape[1]),
        ("zh", "y"),
        split_axis=0,
        concat_axis=0,
        tiled=True,
    )
    summed = jnp.sum(slab_parts.astype(jnp.float32), axis=0)
    ff_here = gate_up.shape[2]
    gate = summed[:, :ff_here]
    up = summed[:, ff_here:]
    return (jax.nn.silu(gate) * up).astype(jnp.bfloat16)


def solution(mesh):
    fine = jax.sharding.Mesh(
        mesh.devices.reshape(2, 4, 4, 2, 2), ("zh", "y", "x", "zl", "core")
    )
    rep = ("zh", "y")
    ten = ("x", "zl", "core")
    placed = (
        P(rep, ten),
        P(rep, None),
        P(rep + ten, None, None),
        P(),
        P(),
        P(),
        P(),
        P(ten, rep),
        P(None, rep),
        P(rep),
        P(rep, None, ten),
    )
    return jax.shard_map(
        per_device, mesh=fine, in_specs=placed, out_specs=P(rep, ten), check_vma=False
    )
```

```python
import jax
import jax.numpy as jnp
import numpy as np
from jax import lax
from jax.sharding import PartitionSpec as P

D = 16384
HD = 128
HEADS = 64
KVH = 4
PAGE = 64
SHARE = 1
ROWS = 128
GROUP = 16


EPSILON = 1e-05


def per_device(
    queries,
    new_kv,
    kv_pool,
    anchor,
    page_table,
    prefix_len,
    turn_rows,
    out_weight,
    residual,
    norm_gain,
    gate_up,
):
    replicas = lax.axis_size("replica")
    tensors = lax.axis_size("tensor")
    replica_idx = lax.axis_index("replica")
    tensor_idx = lax.axis_index("tensor")
    sessions = SHARE * replicas
    heads_local = HEADS // tensors
    pair_width = 2 * HD
    cached_len = tensors * PAGE
    owner_head = np.arange(tensors) * heads_local // GROUP
    from_here = lax.dynamic_slice_in_dim(anchor, replica_idx * SHARE, SHARE, 1)
    table_rows = lax.dynamic_slice_in_dim(page_table, replica_idx * sessions, sessions, 0)
    my_column = lax.dynamic_slice_in_dim(table_rows, tensor_idx, 1, 1)[:, 0]
    page_index = jnp.take(my_column, from_here.reshape(-1), axis=0)
    chosen = jnp.take(kv_pool, page_index, axis=0).reshape(replicas, SHARE, PAGE, KVH, pair_width)
    half = PAGE // 2
    lanes_per_head = tensors // KVH
    outgoing = jnp.transpose(
        chosen.reshape(replicas, 2, half, KVH, pair_width), (0, 3, 1, 2, 4)
    )
    outgoing = jnp.broadcast_to(
        outgoing[:, :, None],
        (replicas, KVH, lanes_per_head // 2, 2, half, pair_width),
    ).reshape(replicas * tensors, SHARE, half, pair_width)
    arrived = lax.all_to_all(
        outgoing, ("replica", "tensor"), split_axis=0, concat_axis=0, tiled=True
    )
    partner = lax.ppermute(arrived, "tensor", [(i, i ^ 1) for i in range(tensors)])
    arrived = jnp.concatenate([arrived, partner], axis=2)
    arrived = arrived.reshape(replicas, tensors, SHARE, PAGE, pair_width)
    prefix_blocks = jnp.transpose(arrived, (0, 2, 1, 3, 4)).reshape(
        sessions, cached_len, pair_width
    )
    kv_group = tensor_idx * heads_local // GROUP
    fresh_pair = lax.dynamic_slice_in_dim(new_kv, kv_group * pair_width, pair_width, 1)
    rows_here = queries.shape[0]
    slot_rows = ROWS // 4
    query_heads = queries.reshape(rows_here, heads_local, HD)
    counts = lax.dynamic_slice_in_dim(turn_rows, replica_idx, 1, 0)[0]
    bounds = jnp.cumsum(counts, dtype=jnp.int32)
    starts = bounds - counts
    row_ids = jnp.arange(rows_here, dtype=jnp.int32)
    row_slot = jnp.sum(
        (row_ids[:, None] >= bounds[None, :]).astype(jnp.int32), axis=1, dtype=jnp.int32
    )
    offsets = jnp.arange(slot_rows, dtype=jnp.int32)
    padded_index = jnp.minimum(starts[:, None] + offsets[None, :], rows_here - 1).reshape(-1)
    slot_queries = jnp.take(query_heads, padded_index, axis=0).reshape(
        sessions, slot_rows, heads_local, HD
    )
    slot_fresh = jnp.take(fresh_pair, padded_index, axis=0).reshape(sessions, slot_rows, pair_width)
    lengths = lax.dynamic_slice_in_dim(prefix_len, replica_idx * sessions, sessions, 0)
    key_ids = jnp.arange(cached_len, dtype=jnp.int32)
    key_pos = (key_ids // PAGE) * PAGE + (key_ids % PAGE + (tensor_idx % 2) * half) % PAGE
    prefix_mask = (key_pos[None, :] < lengths[:, None])[:, None, :]
    fresh_mask = (offsets[None, None, :] <= offsets[None, :, None]) & (
        offsets[None, None, :] < counts[:, None, None]
    )
    score_scale = HD ** (-0.5)
    prefix_scores = (
        jnp.einsum(
            "smhd,skd->hsmk",
            slot_queries,
            prefix_blocks[:, :, :HD],
            preferred_element_type=jnp.float32,
        )
        * score_scale
    )
    fresh_scores = (
        jnp.einsum(
            "smhd,snd->hsmn",
            slot_queries,
            slot_fresh[:, :, :HD],
            preferred_element_type=jnp.float32,
        )
        * score_scale
    )
    prefix_scores = jnp.where(prefix_mask[None], prefix_scores, -jnp.inf)
    fresh_scores = jnp.where(fresh_mask[None], fresh_scores, -jnp.inf)
    row_peak = jnp.maximum(jnp.max(prefix_scores, axis=3), jnp.max(fresh_scores, axis=3))
    prefix_weights = jnp.exp(prefix_scores - row_peak[..., None])
    fresh_weights = jnp.exp(fresh_scores - row_peak[..., None])
    denominator = jnp.sum(prefix_weights, axis=3) + jnp.sum(fresh_weights, axis=3)
    mixed_values = jnp.einsum(
        "hsmk,skd->smhd",
        prefix_weights.astype(jnp.bfloat16),
        prefix_blocks[:, :, HD:],
        preferred_element_type=jnp.float32,
    )
    mixed_values = mixed_values + jnp.einsum(
        "hsmn,snd->smhd",
        fresh_weights.astype(jnp.bfloat16),
        slot_fresh[:, :, HD:],
        preferred_element_type=jnp.float32,
    )
    slot_attended = (mixed_values / jnp.transpose(denominator, (1, 2, 0))[..., None]).astype(
        jnp.bfloat16
    )
    slot_attended = slot_attended.reshape(sessions * slot_rows, heads_local * HD)
    back_index = row_slot * slot_rows + row_ids - jnp.take(starts, row_slot, axis=0)
    attended = jnp.take(slot_attended, back_index, axis=0)
    gathered = lax.all_to_all(
        jnp.broadcast_to(attended[None], (replicas,) + attended.shape),
        "replica",
        split_axis=0,
        concat_axis=0,
        tiled=True,
    ).reshape(replicas * rows_here, attended.shape[1])
    partial_out = jnp.dot(
        gathered,
        out_weight,
        preferred_element_type=jnp.float32,
    )
    all_rows = partial_out.shape[0]
    width = partial_out.shape[1]
    part_rows = all_rows // tensors
    head_parts = lax.all_to_all(
        partial_out.astype(jnp.bfloat16).reshape(tensors, part_rows, width),
        "tensor",
        split_axis=0,
        concat_axis=0,
        tiled=True,
    )
    head_sum = jnp.sum(head_parts.astype(jnp.float32), axis=0)
    my_residual = lax.dynamic_slice_in_dim(residual, tensor_idx * part_rows, part_rows, 0)
    carried = my_residual.astype(jnp.float32) + head_sum
    gain_row = norm_gain.astype(jnp.float32)
    own_squares = jnp.sum(carried * carried, axis=1)
    squares = jnp.sum(
        lax.all_to_all(
            jnp.broadcast_to(own_squares[None], (replicas,) + own_squares.shape),
            "replica",
            split_axis=0,
            concat_axis=0,
            tiled=True,
        ),
        axis=0,
    )
    normed_part = (
        carried * lax.rsqrt(squares / D + EPSILON)[:, None] * gain_row[None, :]
    ).astype(jnp.bfloat16)
    normed = lax.all_gather(normed_part, "tensor", axis=0, tiled=True)
    weights_local = gate_up.reshape(gate_up.shape[0], 2 * gate_up.shape[2])
    slab = jnp.dot(normed, weights_local, preferred_element_type=jnp.float32)
    slab_parts = lax.all_to_all(
        slab.astype(jnp.bfloat16).reshape(replicas, rows_here, slab.shape[1]),
        "replica",
        split_axis=0,
        concat_axis=0,
        tiled=True,
    )
    summed = jnp.sum(slab_parts.astype(jnp.float32), axis=0)
    ff_here = gate_up.shape[2]
    gate = summed[:, :ff_here]
    up = summed[:, ff_here:]
    return (jax.nn.silu(gate) * up).astype(jnp.bfloat16)


def solution(mesh):
    placed = (
        P("replica", "tensor"),
        P("replica", None),
        P(("replica", "tensor"), None, None),
        P(),
        P(),
        P(),
        P(),
        P("tensor", "replica"),
        P(None, "replica"),
        P("replica"),
        P("replica", None, "tensor"),
    )
    return jax.shard_map(
        per_device, mesh=mesh, in_specs=placed, out_specs=P("replica", "tensor"), check_vma=False
    )
```
